32 devices in a mesh: dp: 8 (over y, x, core), tensor: 4 (over z).
Axes of the slice: x: 2, y: 2, z: 4, core: 2. Of those that a mesh axis runs over, the one named last changes fastest.
Arguments:
- block_in: bfloat16 [4096, 2048], P(('dp', 'tensor')), may hold values from -6 to 6
- attn_norm_gain: bfloat16 [2048], P(('dp', 'tensor')), may hold values from 0.5 to 1.5
- query_weight: bfloat16 [2048, 3072], P('dp', 'tensor'), may hold values from -0.125 to 0.125
- kv_down_weight: bfloat16 [2048, 576], P(('dp', 'tensor')), may hold values from -0.125 to 0.125
- latent_gain: bfloat16 [512], P(('dp', 'tensor')), may hold values from 0.5 to 1.5
- kv_up_weight: bfloat16 [512, 4096], P('dp', 'tensor'), may hold values from -0.25 to 0.25
- output_weight: bfloat16 [2048, 2048], P('tensor', 'dp'), may hold values from -0.5 to 0.5
- ffn_norm_gain: bfloat16 [2048], P(('dp', 'tensor')), may hold values from 0.5 to 1.5
- router_weight: bfloat16 [2048, 64], P(('dp', 'tensor')), may hold values from -0.125 to 0.125
- expert_ids: int32 [4096, 6], P('dp'), may hold values from 0 to 63, all different within a row; in each aligned block of 512 rows (0 to 511, 512 to 1023, ...) at most 96 rows name the same one
- shared_gate_weight: bfloat16 [2048, 2816], P('dp', 'tensor'), may hold values from -0.125 to 0.125
- shared_up_weight: bfloat16 [2048, 2816], P('dp', 'tensor'), may hold values from -0.125 to 0.125
- shared_down_weight: bfloat16 [2816, 2048], P('tensor', 'dp'), may hold values from -0.109375 to 0.109375
- expert_gate_weight: bfloat16 [8, 2048, 1408], P(None, 'dp', 'tensor'), may hold values from -0.125 to 0.125
- expert_up_weight: bfloat16 [8, 2048, 1408], P(None, 'dp', 'tensor'), may hold values from -0.125 to 0.125
- expert_down_weight: bfloat16 [8, 1408, 2048], P(None, 'tensor', 'dp'), may hold values from -2.5 to 2.5
- out_grad: bfloat16 [4096, 2048], P(('dp', 'tensor')), may hold values from -6 to 6
Outputs:
- block_out: bfloat16 [4096, 2048], P(('dp', 'tensor'))
- input_grad: float32 [4096, 2048], P(('dp', 'tensor'))
- attn_norm_gain_grad: float32 [2048], P(('dp', 'tensor'))
- query_weight_grad: float32 [2048, 3072], P('dp', 'tensor')
- kv_down_weight_grad: float32 [2048, 576], P(('dp', 'tensor'))
- latent_gain_grad: float32 [512], P(('dp', 'tensor'))
- kv_up_weight_grad: float32 [512, 4096], P('dp', 'tensor')
- output_weight_grad: float32 [2048, 2048], P('tensor', 'dp')
- ffn_norm_gain_grad: float32 [2048], P(('dp', 'tensor'))
- router_weight_grad: float32 [2048, 64], P(('dp', 'tensor'))
- shared_gate_weight_grad: float32 [2048, 2816], P('dp', 'tensor')
- shared_up_weight_grad: float32 [2048, 2816], P('dp', 'tensor')
- shared_down_weight_grad: float32 [2816, 2048], P('tensor', 'dp')
- expert_gate_weight_grad: float32 [8, 2048, 1408], P(None, 'dp', 'tensor')
- expert_up_weight_grad: float32 [8, 2048, 1408], P(None, 'dp', 'tensor')
- expert_down_weight_grad: float32 [8, 1408, 2048], P(None, 'tensor', 'dp')
The draws below stay inside these ranges and needn't reach their ends.
Inputs may be any that keep to these rules, and one draw needn't show every extreme that they name: `expert_ids`: each row names 6 different experts. Of the 512 rows of one index of dp, at most 96 name the same expert, a bound that some block reaches of them.
All inputs are finite; a program needn't handle non-finite values.
Results may differ from the reference program's by a relative error of at most 0.02.
Values may be sent and summed in bfloat16 or wider, within the bound.
No kernel may reach another device: no remote copies, remote signals or barrier semaphores. Data moves between devices by JAX's collectives and lax.ppermute only.
A program may use at most 192 MiB of HBM per device.

```python
import math
import jax
import jax.numpy as jnp
import numpy as np
from jax import lax

D = 2048
H = 16
NOPE = 128
ROPE = 64
VDIM = 128
LATENT = 512
EXPERTS = 64
TOPK = 6
FF = 1408
SHARED = 2816
ACTIVE = 8
SEQ = 512
TOK_DP = 512
CAP = 96
TOKENS = 4096


def level_of(key, dims, pieces, smallest, high):
    gain = 1.0
    for dim, parts in pieces:
        heights = jax.random.uniform(jax.random.fold_in(jax.random.fold_in(key, 6), dim), (parts,), jnp.float32, smallest / len(pieces), high / len(pieces))
        gain = gain * jnp.repeat(jnp.exp(heights), dims[dim] // parts).reshape((-1,) + (1,) * (len(dims) - 1 - dim))
    return gain


def routed_block(rng, own, number, rows, count, top, reach, slope):
    sequence = jax.random.permutation(rng, count)
    heavy_load, common = load_shares(count, rows * top, reach, slope, True), load_shares(count, rows * top, reach, slope, False)
    places = jnp.arange(count)

    def named(lengths, rotation):
        used = int((lengths > 0).sum())
        fixed = max(1, used // 4)
        shifted = fixed + (places - fixed + rotation * (used - fixed)) % max(1, count - fixed)
        return jnp.zeros((count,), jnp.int32).at[sequence[jnp.where(places < fixed, places, shifted)]].set(jnp.asarray(lengths, jnp.int32))

    lengths = jnp.where(number % 4 == 0, named(heavy_load, number // 4), named(common, number - number // 4 - 1))
    mixed = jax.random.permutation(jax.random.fold_in(own, 3), count)
    donor, sink = mixed[0:count // 2 * 2:2], mixed[1:count // 2 * 2:2]
    room = jnp.minimum(lengths[donor] - 1, reach - lengths[sink]) // 2
    room = jnp.where((donor == sequence[0]) | (sink == sequence[0]) | (lengths[sink] == 0), 0, jnp.maximum(room, 0))
    shifted = jax.random.randint(jax.random.fold_in(own, 4), (count // 2,), 0, 1 << 20) % (room + 1)
    lengths = lengths.at[donor].add(-shifted).at[sink].add(shifted)
    labels = jnp.searchsorted(jnp.cumsum(lengths), jnp.arange(rows * top), side="right").astype(jnp.int32)
    table = labels.reshape(top, rows).T
    table = table[jax.random.permutation(jax.random.fold_in(own, 1), rows)]
    rotation = jax.random.randint(jax.random.fold_in(own, 2), (rows, 1), 0, top)
    return jnp.take_along_axis(table, (jnp.arange(top)[None, :] + rotation) % top, axis=1)


def load_shares(amount, total, most, slope, full):
    loads = [(1 << 20) // math.isqrt(rank ** slope) + 1 for rank in range(1, amount + 1)]
    largest = most if full else min(most, max(-(-total // amount), total * loads[0] // sum(loads)))
    least = 1 if total - largest >= amount - 1 else 0
    given, surplus = [largest] + [least] * (amount - 1), total - largest - least * (amount - 1)
    while surplus > 0:
        movable = [i for i in range(1, amount) if given[i] < largest] or [i for i in range(1, amount) if given[i] < most]
        whole, remaining = sum([loads[i] for i in movable]), surplus
        for i in movable:
            more = min(most - given[i], max(1, remaining * loads[i] // whole), surplus)
            given[i] = given[i] + more
            surplus = surplus - more
    return np.array(given)


def bell_draw(key, shape, scale, bound, cuts=(), kind=jnp.bfloat16):
    result = jax.random.normal(key, shape, jnp.float32) * scale
    if len(cuts) > 0:
        result = level_of(key, shape, cuts, -0.22, 0.18) * result
    return jnp.clip(result, min=-bound, max=bound).astype(kind)


def setup_inputs(seed: int = 0) -> dict:
    splits = jax.random.split(jax.random.key(seed), 18)
    block_in = bell_draw(splits[0], (TOKENS, D), 1.0, 6.0, ((0, 32),))
    attn_norm_gain = jnp.clip(1.0 + 0.1 * jax.random.normal(splits[1], (D,), jnp.float32), 0.5, 1.5).astype(jnp.bfloat16)
    query_weight = bell_draw(splits[2], (D, H * (NOPE + ROPE)), D ** -0.5, 0.125, ((0, 8), (1, 4)))
    kv_down_weight = bell_draw(splits[3], (D, LATENT + ROPE), D ** -0.5, 0.125, ((0, 32),))
    latent_gain = jnp.clip(1.0 + 0.1 * jax.random.normal(splits[4], (LATENT,), jnp.float32), 0.5, 1.5).astype(jnp.bfloat16)
    kv_up_weight = bell_draw(splits[5], (LATENT, H * (NOPE + VDIM)), LATENT ** -0.5, 0.25, ((0, 8), (1, 4)))
    output_weight = bell_draw(splits[6], (H * VDIM, D), VDIM ** -0.5, 0.5, ((0, 4), (1, 8)))
    ffn_norm_gain = jnp.clip(1.0 + 0.1 * jax.random.normal(splits[7], (D,), jnp.float32), 0.5, 1.5).astype(jnp.bfloat16)
    router_weight = bell_draw(splits[8], (D, EXPERTS), D ** -0.5, 0.125, ((0, 32),))
    expert_ids_keys = jax.random.split(jax.random.fold_in(splits[9], 1), TOKENS // TOK_DP)
    expert_ids_turns = jax.random.permutation(jax.random.fold_in(splits[9], 3), TOKENS // TOK_DP)
    expert_ids = jax.vmap(lambda own, number: routed_block(jax.random.fold_in(splits[9], 2), own, number, TOK_DP, EXPERTS, TOPK, CAP, 2))(expert_ids_keys, expert_ids_turns).reshape((TOKENS, TOPK))
    shared_gate_weight = bell_draw(splits[10], (D, SHARED), D ** -0.5, 0.125, ((0, 8), (1, 4)))
    shared_up_weight = bell_draw(splits[11], (D, SHARED), D ** -0.5, 0.125, ((0, 8), (1, 4)))
    shared_down_weight = bell_draw(splits[12], (SHARED, D), SHARED ** -0.5, 0.109375, ((0, 4), (1, 8)))
    expert_gate_weight = bell_draw(splits[13], (ACTIVE, D, FF), D ** -0.5, 0.125, ((1, 8), (2, 4)))
    expert_up_weight = bell_draw(splits[14], (ACTIVE, D, FF), D ** -0.5, 0.125, ((1, 8), (2, 4)))
    expert_down_weight = bell_draw(splits[15], (ACTIVE, FF, D), (max(FF // 256, 1)) ** -0.5, 2.5, ((1, 4), (2, 8)))
    out_grad = bell_draw(splits[16], (TOKENS, D), 1.0, 6.0, ((0, 32),))
    return {"block_in": block_in, "attn_norm_gain": attn_norm_gain, "query_weight": query_weight, "kv_down_weight": kv_down_weight, "latent_gain": latent_gain, "kv_up_weight": kv_up_weight, "output_weight": output_weight, "ffn_norm_gain": ffn_norm_gain, "router_weight": router_weight, "expert_ids": expert_ids, "shared_gate_weight": shared_gate_weight, "shared_up_weight": shared_up_weight, "shared_down_weight": shared_down_weight, "expert_gate_weight": expert_gate_weight, "expert_up_weight": expert_up_weight, "expert_down_weight": expert_down_weight, "out_grad": out_grad}


EPSILON = 1e-06
NEGATIVE = -1e+30

def matmul(left, right):
    return jnp.dot(left, right, preferred_element_type=jnp.float32)

def rms_scale(values):
    return lax.rsqrt(lax.optimization_barrier(jnp.mean(values * values, axis=-1, keepdims=True)) + EPSILON)

def norm_back(grad_normed, normed, scale):
    return scale * (grad_normed - normed * lax.optimization_barrier(jnp.mean(grad_normed * normed, axis=-1, keepdims=True)))

def silu_grad(values):
    sigma = jax.nn.sigmoid(values)
    return sigma * (1.0 + values * (1.0 - sigma))

def rope_tables(count):
    position = (jnp.arange(count) % SEQ).astype(jnp.float32)
    halfway = ROPE // 2
    inverse = jnp.exp(-jnp.log(10000.0) * jnp.arange(halfway).astype(jnp.float32) / halfway)
    angles = position[:, None] * inverse[None, :]
    return (jnp.cos(angles), jnp.sin(angles))

def rotate(values, cosine, sine):
    halfway = ROPE // 2
    first, second = (values[..., :halfway], values[..., halfway:])
    return jnp.concatenate([first * cosine - second * sine, first * sine + second * cosine], axis=-1)

def unrotate(grads, cosine, sine):
    halfway = ROPE // 2
    first, second = (grads[..., :halfway], grads[..., halfway:])
    return jnp.concatenate([first * cosine + second * sine, second * cosine - first * sine], axis=-1)

def causal_scores(query_nope, query_rope, key_nope, key_rope):
    wide = jnp.float32
    scores = jnp.einsum('qhd,khd->hqk', query_nope.astype(wide), key_nope.astype(wide))
    scores = scores + jnp.einsum('qhd,kd->hqk', query_rope.astype(wide), key_rope.astype(wide))
    length = query_nope.shape[0]
    causal = jnp.arange(length)[:, None] >= jnp.arange(length)[None, :]
    return jnp.where(causal[None], scores * (NOPE + ROPE) ** (-0.5), NEGATIVE)

def attend_forward(blocks):
    query_nope, query_rope, key_nope, key_rope, values = blocks
    scores = causal_scores(query_nope, query_rope, key_nope, key_rope)
    logsum = jax.nn.logsumexp(scores, axis=-1)
    probs = jnp.exp(scores - logsum[..., None]).astype(jnp.bfloat16)
    mixed = jnp.einsum('hqk,khd->qhd', probs.astype(jnp.float32), values.astype(jnp.float32))
    return (mixed.astype(jnp.bfloat16), logsum)

def attend_backward(blocks):
    query_nope, query_rope, key_nope, key_rope, values, mixed, mixed_grad, logsum = blocks
    wide = jnp.float32
    scores = causal_scores(query_nope, query_rope, key_nope, key_rope)
    probs_full = jnp.exp(scores - logsum[..., None])
    probs = probs_full.astype(jnp.bfloat16).astype(wide)
    values_grad = jnp.einsum('hqk,qhd->khd', probs, mixed_grad.astype(wide))
    probs_grad = jnp.einsum('qhd,khd->hqk', mixed_grad.astype(wide), values.astype(wide))
    delta = jnp.einsum('qhd,qhd->hq', mixed_grad.astype(wide), mixed.astype(wide))
    score_grad = (probs_full * (probs_grad - delta[..., None]) * (NOPE + ROPE) ** (-0.5)).astype(jnp.bfloat16).astype(wide)
    query_nope_grad = jnp.einsum('hqk,khd->qhd', score_grad, key_nope.astype(wide))
    query_rope_grad = jnp.einsum('hqk,kd->qhd', score_grad, key_rope.astype(wide))
    key_nope_grad = jnp.einsum('hqk,qhd->khd', score_grad, query_nope.astype(wide))
    key_rope_grad = jnp.einsum('hqk,qhd->kd', score_grad, query_rope.astype(wide))
    return (query_nope_grad, query_rope_grad, key_nope_grad, key_rope_grad, values_grad)

def reference(block_in, attn_norm_gain, query_weight, kv_down_weight, latent_gain, kv_up_weight, output_weight, ffn_norm_gain, router_weight, expert_ids, shared_gate_weight, shared_up_weight, shared_down_weight, expert_gate_weight, expert_up_weight, expert_down_weight, out_grad):
    wide = jnp.float32
    narrow = jnp.bfloat16
    count = block_in.shape[0]
    nseqs = count // SEQ
    residual_in = block_in.astype(wide)
    scale_one = rms_scale(residual_in)
    normed_one = residual_in * scale_one
    gain_one = attn_norm_gain.astype(wide)
    hidden_one = (normed_one * gain_one).astype(narrow)
    latent_in = matmul(hidden_one, kv_down_weight).astype(narrow)
    compressed = latent_in[:, :LATENT].astype(wide)
    scale_lat = rms_scale(compressed)
    normed_lat = compressed * scale_lat
    gain_lat = latent_gain.astype(wide)
    latent = (normed_lat * gain_lat).astype(narrow)
    cosine, sine = rope_tables(count)
    key_rope = rotate(latent_in[:, LATENT:].astype(wide), cosine, sine).astype(narrow)
    query = matmul(hidden_one, query_weight).reshape(count, H, NOPE + ROPE)
    query_nope = query[..., :NOPE].astype(narrow)
    query_rope = rotate(query[..., NOPE:], cosine[:, None, :], sine[:, None, :]).astype(narrow)
    keyvalue = matmul(latent, kv_up_weight).astype(narrow).reshape(count, H, NOPE + VDIM)
    key_nope = keyvalue[..., :NOPE]
    values = keyvalue[..., NOPE:]

    def by_seq(array):
        return array.reshape((nseqs, SEQ) + array.shape[1:])
    mixed, logsum = lax.map(attend_forward, (by_seq(query_nope), by_seq(query_rope), by_seq(key_nope), by_seq(key_rope), by_seq(values)))
    mixed = mixed.reshape(count, H * VDIM)
    after_attn = residual_in + matmul(mixed, output_weight)
    scale_two = rms_scale(after_attn)
    normed_two = after_attn * scale_two
    gain_two = ffn_norm_gain.astype(wide)
    hidden_two = (normed_two * gain_two).astype(narrow)
    route_prob = jax.nn.softmax(matmul(hidden_two, router_weight), axis=-1)
    chosen = jnp.any(expert_ids[:, :, None] == jnp.arange(ACTIVE, dtype=jnp.int32)[None, None, :], axis=1)
    gate = jnp.where(chosen, route_prob[:, :ACTIVE], 0.0)
    shared_a = matmul(hidden_two, shared_gate_weight)
    shared_b = matmul(hidden_two, shared_up_weight)
    shared_hidden = (jax.nn.silu(shared_a) * shared_b).astype(narrow)
    output_sum = after_attn + matmul(shared_hidden, shared_down_weight)
    limit = CAP * (count // TOK_DP)
    saved = []
    for expert in range(ACTIVE):
        found = jnp.nonzero(chosen[:, expert], size=limit, fill_value=0)[0].astype(jnp.int32)
        filled = jnp.arange(limit) < jnp.sum(chosen[:, expert].astype(jnp.int32))
        weight = jnp.where(filled, gate[found, expert], 0.0)
        tokens_in = hidden_two[found]
        expert_a = matmul(tokens_in, expert_gate_weight[expert])
        expert_b = matmul(tokens_in, expert_up_weight[expert])
        expert_hidden = (jax.nn.silu(expert_a) * expert_b).astype(narrow)
        routed = matmul(expert_hidden, expert_down_weight[expert])
        output_sum = output_sum.at[found].add(weight[:, None] * routed)
        saved.append((found, filled, weight, tokens_in, expert_a, expert_b, expert_hidden))
    block_out = output_sum.astype(narrow)
    shared_up_grad = matmul(out_grad, shared_down_weight.T)
    shared_a_grad = (shared_up_grad * shared_b * silu_grad(shared_a)).astype(narrow)
    shared_b_grad = (shared_up_grad * jax.nn.silu(shared_a)).astype(narrow)
    shared_down_grad = matmul(shared_hidden.T, out_grad)
    shared_gate_grad = matmul(hidden_two.T, shared_a_grad)
    shared_up_wgrad = matmul(hidden_two.T, shared_b_grad)
    hidden_two_grad = matmul(shared_a_grad, shared_gate_weight.T) + matmul(shared_b_grad, shared_up_weight.T)
    gate_grad = jnp.zeros((count, ACTIVE), wide)
    gate_list, upw_list, down_list = ([], [], [])
    for expert in range(ACTIVE):
        found, filled, weight, tokens_in, expert_a, expert_b, expert_hidden = saved[expert]
        grad_in = out_grad[found]
        expert_up_grad = matmul(grad_in, expert_down_weight[expert].T)
        per_slot = jnp.where(filled, lax.optimization_barrier(jnp.sum(expert_up_grad * expert_hidden.astype(wide), axis=-1)), 0.0)
        gate_grad = gate_grad.at[found, expert].add(per_slot)
        hidden_grad = weight[:, None] * expert_up_grad
        expert_a_grad = (hidden_grad * expert_b * silu_grad(expert_a)).astype(narrow)
        expert_b_grad = (hidden_grad * jax.nn.silu(expert_a)).astype(narrow)
        scaled_hidden = (weight[:, None] * expert_hidden.astype(wide)).astype(narrow)
        down_list.append(matmul(scaled_hidden.T, grad_in))
        gate_list.append(matmul(tokens_in.T, expert_a_grad))
        upw_list.append(matmul(tokens_in.T, expert_b_grad))
        back = matmul(expert_a_grad, expert_gate_weight[expert].T) + matmul(expert_b_grad, expert_up_weight[expert].T)
        hidden_two_grad = hidden_two_grad.at[found].add(back)
    prob_grad = jnp.concatenate([gate_grad, jnp.zeros((count, EXPERTS - ACTIVE), wide)], axis=-1)
    logit_grad = (route_prob * (prob_grad - lax.optimization_barrier(jnp.sum(route_prob * prob_grad, axis=-1, keepdims=True)))).astype(narrow)
    router_grad = matmul(hidden_two.T, logit_grad)
    hidden_two_grad = hidden_two_grad + matmul(logit_grad, router_weight.T)
    gain_two_grad = lax.optimization_barrier(jnp.sum(hidden_two_grad * normed_two, axis=0))
    after_attn_grad = out_grad.astype(wide) + norm_back(hidden_two_grad * gain_two, normed_two, scale_two)
    residual_low = after_attn_grad.astype(narrow)
    output_grad = matmul(mixed.T, residual_low)
    mixed_grad = matmul(residual_low, output_weight.T).astype(narrow).reshape(count, H, VDIM)
    grads = lax.map(attend_backward, (by_seq(query_nope), by_seq(query_rope), by_seq(key_nope), by_seq(key_rope), by_seq(values), by_seq(mixed.reshape(count, H, VDIM)), by_seq(mixed_grad), logsum))
    query_nope_grad, query_rope_grad, key_nope_grad, key_rope_grad, values_grad = [part.reshape((count,) + part.shape[2:]) for part in grads]
    query_rope_back = unrotate(query_rope_grad, cosine[:, None, :], sine[:, None, :])
    query_grad = jnp.concatenate([query_nope_grad, query_rope_back], axis=-1).astype(narrow).reshape(count, H * (NOPE + ROPE))
    keyvalue_grad = jnp.concatenate([key_nope_grad, values_grad], axis=-1).astype(narrow).reshape(count, H * (NOPE + VDIM))
    kv_up_grad = matmul(latent.T, keyvalue_grad)
    latent_grad = matmul(keyvalue_grad, kv_up_weight.T)
    gain_lat_grad = lax.optimization_barrier(jnp.sum(latent_grad * normed_lat, axis=0))
    compressed_grad = norm_back(latent_grad * gain_lat, normed_lat, scale_lat)
    key_rope_back = unrotate(key_rope_grad, cosine, sine)
    latent_in_grad = jnp.concatenate([compressed_grad, key_rope_back], axis=-1).astype(narrow)
    query_wgrad = matmul(hidden_one.T, query_grad)
    kv_down_grad = matmul(hidden_one.T, latent_in_grad)
    hidden_one_grad = matmul(query_grad, query_weight.T) + matmul(latent_in_grad, kv_down_weight.T)
    gain_one_grad = lax.optimization_barrier(jnp.sum(hidden_one_grad * normed_one, axis=0))
    input_grad = after_attn_grad + norm_back(hidden_one_grad * gain_one, normed_one, scale_one)
    return (block_out, input_grad, gain_one_grad, query_wgrad, kv_down_grad, gain_lat_grad, kv_up_grad, output_grad, gain_two_grad, router_grad, shared_gate_grad, shared_up_wgrad, shared_down_grad, jnp.stack(gate_list), jnp.stack(upw_list), jnp.stack(down_list))
```

```python
import jax
import jax.numpy as jnp
from jax import lax
from jax.sharding import PartitionSpec as P

NOPE = 128
ROPE = 64
VDIM = 128
LATENT = 512
ACTIVE = 8
SEQ = 512
CAP = 96


EPSILON = 1e-06
NEGATIVE = -1e30


def matmul(left, right):
    return jnp.dot(left, right, preferred_element_type=jnp.float32)


def left_dot(left, right):
    return lax.dot_general(
        left, right, (((0,), (0,)), ((), ())), preferred_element_type=jnp.float32
    )


def right_dot(left, right):
    return lax.dot_general(
        left, right, (((left.ndim - 1,), (1,)), ((), ())), preferred_element_type=jnp.float32
    )


def einsum32(form, left, right):
    return jnp.einsum(form, left, right, preferred_element_type=jnp.float32)


def rms_scale(values):
    return lax.rsqrt(jnp.mean(values * values, axis=-1, keepdims=True) + EPSILON)


def norm_back(grad_normed, normed, scale):
    return scale * (grad_normed - normed * jnp.mean(grad_normed * normed, axis=-1, keepdims=True))


def silu_grad(values):
    sigma = jax.nn.sigmoid(values)
    return sigma * (1.0 + values * (1.0 - sigma))


def rope_tables(position):
    halfway = ROPE // 2
    inverse = jnp.exp(-jnp.log(10000.0) * jnp.arange(halfway).astype(jnp.float32) / halfway)
    angles = position[:, None] * inverse[None, :]
    return (jnp.cos(angles), jnp.sin(angles))


def rotate(values, cosine, sine):
    halfway = ROPE // 2
    first, second = (values[..., :halfway], values[..., halfway:])
    return jnp.concatenate(
        [first * cosine - second * sine, first * sine + second * cosine], axis=-1
    )


def unrotate(grads, cosine, sine):
    halfway = ROPE // 2
    first, second = (grads[..., :halfway], grads[..., halfway:])
    return jnp.concatenate(
        [first * cosine + second * sine, second * cosine - first * sine], axis=-1
    )


def send_tensor(values, step):
    count = lax.axis_size("tensor")
    return lax.ppermute(values, "tensor", [(i, (i + step) % count) for i in range(count)])


def halves(values):
    middle = values.shape[0] // 2
    return [values[:middle], values[middle:]]


def gather_tensor(own):
    pieces = halves(own)
    found = [list(pieces)]
    for _ in range(lax.axis_size("tensor") - 1):
        pieces = [send_tensor(piece, -1) for piece in pieces]
        found.append(list(pieces))
    return jnp.concatenate([piece for row in found for piece in row], axis=0)


def scatter_tensor(share):
    count = lax.axis_size("tensor")
    blocks = share.reshape((count, share.shape[0] // count) + share.shape[1:])
    sums = [piece.astype(jnp.bfloat16) for piece in halves(blocks[count - 1])]
    for step in range(count - 2, -1, -1):
        sums = [send_tensor(piece.astype(jnp.bfloat16), 1) for piece in sums]
        sums = [
            piece.astype(jnp.float32) + more.astype(jnp.float32)
            for piece, more in zip(sums, halves(blocks[step]))
        ]
    return jnp.concatenate(sums, axis=0)


def shift_blocks(share):
    count = lax.axis_size("tensor")
    index = lax.axis_index("tensor")
    twice = share.reshape((count, share.shape[0] // count) + share.shape[1:])
    twice = jnp.concatenate([twice, twice], axis=0)
    return exchange(lax.dynamic_slice_in_dim(twice, (count - index) % count, count, 0), "tensor")


def exchange(values, axes):
    return lax.all_to_all(values, axes, split_axis=0, concat_axis=0, tiled=True)


def dp_orders():
    count = lax.axis_size("dp")
    masks = [1 << k for k in range(count.bit_length() - 1)]
    return (masks[1:] + masks[:1], masks[:0:-1] + masks[:1])


def swap_dp(values, mask):
    count = lax.axis_size("dp")
    return lax.ppermute(values, "dp", [(i, i ^ mask) for i in range(count)])


def axis_of(mask):
    return lax.axis_size("dp").bit_length() - 1 - mask.bit_length()


def gather_dp(own, order):
    count = lax.axis_size("dp")
    index = lax.axis_index("dp")
    current = own.reshape((1,) * (count.bit_length() - 1) + own.shape)
    for mask in order:
        other = swap_dp(current, mask)
        high = (index & mask) > 0
        current = jnp.concatenate(
            [jnp.where(high, other, current), jnp.where(high, current, other)], axis=axis_of(mask)
        )
    return current.reshape((count,) + own.shape)


def scatter_dp(blocks, order):
    count = lax.axis_size("dp")
    index = lax.axis_index("dp")
    own = blocks.shape[1:]
    current = blocks.reshape((2,) * (count.bit_length() - 1) + own)
    for mask in order[::-1]:
        high = ((index & mask) > 0).astype(jnp.int32)
        axis = axis_of(mask)
        keep = lax.dynamic_slice_in_dim(current, high, 1, axis)
        give = lax.dynamic_slice_in_dim(current, 1 - high, 1, axis)
        got = swap_dp(give.astype(jnp.bfloat16), mask)
        current = keep.astype(jnp.float32) + got.astype(jnp.float32)
    return current.reshape(own)


def causal_scores(query_nope, query_rope, key_nope, key_rope, seen):
    scores = einsum32("qhd,khd->hqk", query_nope, key_nope)
    scores = scores + einsum32("qhd,kd->hqk", query_rope, key_rope)
    return jnp.where(seen[None], scores * (NOPE + ROPE) ** (-0.5), NEGATIVE)


def attend_forward(query_nope, query_rope, key_nope, key_rope, values, seen):
    scores = causal_scores(query_nope, query_rope, key_nope, key_rope, seen)
    logsum = jax.nn.logsumexp(scores, axis=-1)
    probs = jnp.exp(scores - logsum[..., None]).astype(jnp.bfloat16)
    return (einsum32("hqk,khd->qhd", probs, values).astype(jnp.bfloat16), logsum)


def attend_backward(
    query_nope, query_rope, key_nope, key_rope, values, mixed, mixed_grad, logsum, seen
):
    scores = causal_scores(query_nope, query_rope, key_nope, key_rope, seen)
    probs_full = jnp.exp(scores - logsum[..., None])
    probs = probs_full.astype(jnp.bfloat16)
    values_grad = einsum32("hqk,qhd->khd", probs, mixed_grad)
    probs_grad = einsum32("qhd,khd->hqk", mixed_grad, values)
    delta = einsum32("qhd,qhd->hq", mixed_grad, mixed)
    score_grad = (probs_full * (probs_grad - delta[..., None]) * (NOPE + ROPE) ** (-0.5)).astype(
        jnp.bfloat16
    )
    query_nope_grad = einsum32("hqk,khd->qhd", score_grad, key_nope)
    query_rope_grad = einsum32("hqk,kd->qhd", score_grad, key_rope)
    key_nope_grad = einsum32("hqk,qhd->khd", score_grad, query_nope)
    key_rope_grad = einsum32("hqk,qhd->kd", score_grad, query_rope)
    return (query_nope_grad, query_rope_grad, key_nope_grad, key_rope_grad, values_grad)


def per_device(
    block_in,
    attn_norm_gain,
    query_weight,
    kv_down_weight,
    latent_gain,
    kv_up_weight,
    output_weight,
    ffn_norm_gain,
    router_weight,
    expert_ids,
    shared_gate_weight,
    shared_up_weight,
    shared_down_weight,
    expert_gate_weight,
    expert_up_weight,
    expert_down_weight,
    out_grad,
):
    wide = jnp.float32
    narrow = jnp.bfloat16
    own_rows = block_in.shape[0]
    width = block_in.shape[1]
    dp_count = lax.axis_size("dp")
    tensor_count = lax.axis_size("tensor")
    tensor_index = lax.axis_index("tensor")
    group = own_rows * tensor_count
    owner_count = dp_count // ACTIVE
    slot_piece = CAP // owner_count
    slots = ACTIVE * CAP
    both = ("dp", "tensor")
    first_order, second_order = dp_orders()

    gains = jnp.concatenate([attn_norm_gain, ffn_norm_gain, latent_gain])
    gains = exchange(
        jnp.broadcast_to(gains[None], (dp_count * tensor_count, gains.shape[0])), both
    ).astype(wide)
    split_one = attn_norm_gain.shape[0]
    gain_one = gains[:, :split_one].reshape(-1)
    gain_two = gains[:, split_one : 2 * split_one].reshape(-1)
    gain_lat = gains[:, 2 * split_one :].reshape(-1)

    all_in = gather_tensor(block_in)
    small = jnp.concatenate([kv_down_weight, router_weight], axis=1)
    small = exchange(jnp.broadcast_to(small[None], (tensor_count,) + small.shape), "tensor")
    query_full = gather_dp(query_weight, first_order).reshape(width, -1)
    kv_up_full = gather_dp(kv_up_weight, second_order).reshape(LATENT, -1)
    small = gather_dp(small, second_order).reshape(width, -1)
    kv_down = small[:, : LATENT + ROPE]
    router = small[:, LATENT + ROPE :]
    output_full = jnp.moveaxis(gather_dp(output_weight, second_order), 0, 1).reshape(
        output_weight.shape[0], width
    )
    grad_all = gather_tensor(out_grad)

    heads = query_full.shape[1] // (NOPE + ROPE)
    residual_all = all_in.astype(wide)
    scale_all = rms_scale(residual_all)
    hidden_one = (residual_all * scale_all * gain_one).astype(narrow)
    latent_in = matmul(hidden_one, kv_down).astype(narrow)
    compressed = latent_in[:, :LATENT].astype(wide)
    scale_lat = rms_scale(compressed)
    normed_lat = compressed * scale_lat
    latent = (normed_lat * gain_lat).astype(narrow)
    place = (jnp.arange(group) + tensor_index * own_rows) % group
    position = (place % SEQ).astype(wide)
    sequence = place // SEQ
    seen = (place[:, None] >= place[None, :]) & (sequence[:, None] == sequence[None, :])
    cosine, sine = rope_tables(position)
    key_rope = rotate(latent_in[:, LATENT:].astype(wide), cosine, sine).astype(narrow)
    query = matmul(hidden_one, query_full).reshape(group, heads, NOPE + ROPE)
    query_nope = query[..., :NOPE].astype(narrow)
    query_rope = rotate(query[..., NOPE:], cosine[:, None, :], sine[:, None, :]).astype(narrow)
    keyvalue = matmul(latent, kv_up_full).astype(narrow).reshape(group, heads, NOPE + VDIM)
    key_nope = keyvalue[..., :NOPE]
    values = keyvalue[..., NOPE:]
    mixed, logsum = attend_forward(query_nope, query_rope, key_nope, key_rope, values, seen)
    mixed_flat = mixed.reshape(group, heads * VDIM)
    attn_own = scatter_tensor(matmul(mixed_flat, output_full))

    residual_in = block_in.astype(wide)
    after_attn = residual_in + attn_own
    scale_two = rms_scale(after_attn)
    normed_two = after_attn * scale_two
    hidden_two_own = (normed_two * gain_two).astype(narrow)
    hidden_two = gather_tensor(hidden_two_own)

    shared_gate = gather_dp(shared_gate_weight, first_order).reshape(width, -1)
    shared_up = gather_dp(shared_up_weight, second_order).reshape(width, -1)
    shared_down = jnp.moveaxis(gather_dp(shared_down_weight, first_order), 0, 1).reshape(
        shared_down_weight.shape[0], width
    )
    slabs = jnp.concatenate(
        [expert_gate_weight, expert_up_weight, jnp.swapaxes(expert_down_weight, 1, 2)], axis=1
    )
    slabs = exchange(jnp.repeat(slabs, owner_count, axis=0), "dp")
    rows_dp = expert_gate_weight.shape[1]
    gate_here = slabs[:, :rows_dp].reshape(width, -1)
    up_here = slabs[:, rows_dp : 2 * rows_dp].reshape(width, -1)
    down_here = slabs[:, 2 * rows_dp :].reshape(width, -1)

    ids = jnp.concatenate([expert_ids, expert_ids], axis=0)
    ids = lax.dynamic_slice_in_dim(ids, tensor_index * own_rows, group, 0)
    chosen = jnp.any(ids[:, :, None] == jnp.arange(ACTIVE, dtype=jnp.int32)[None, None, :], axis=1)
    ranks = jnp.cumsum(chosen.astype(jnp.int32), axis=0) - 1
    places = (ranks[:, :, None] == jnp.arange(CAP, dtype=jnp.int32)[None, None, :]) & chosen[
        :, :, None
    ]
    pick = places.astype(narrow).reshape(group, slots)
    grad_in = left_dot(pick, grad_all).astype(narrow)
    grad_here = exchange(grad_in.reshape(dp_count, slot_piece, width), "dp").reshape(-1, width)
    tokens_in = left_dot(pick, hidden_two).astype(narrow)
    rows_here = exchange(tokens_in.reshape(dp_count, slot_piece, width), "dp").reshape(-1, width)
    route_prob = jax.nn.softmax(matmul(hidden_two, router), axis=-1)
    gate = jnp.where(chosen, route_prob[:, :ACTIVE], 0.0)
    weight = jnp.sum(jnp.where(places, gate[:, :, None], 0.0), axis=0)
    weight_here = exchange(weight.reshape(dp_count, slot_piece), "dp").reshape(-1)

    shared_a = matmul(hidden_two, shared_gate)
    shared_b = matmul(hidden_two, shared_up)
    shared_hidden = (jax.nn.silu(shared_a) * shared_b).astype(narrow)
    shared_up_grad = right_dot(grad_all, shared_down)
    shared_a_grad = (shared_up_grad * shared_b * silu_grad(shared_a)).astype(narrow)
    shared_b_grad = (shared_up_grad * jax.nn.silu(shared_a)).astype(narrow)
    hidden_two_share = right_dot(shared_a_grad, shared_gate) + right_dot(shared_b_grad, shared_up)
    moe_share = matmul(shared_hidden, shared_down)
    shared_down_grad = left_dot(shared_hidden, grad_all)
    shared_gate_grad = left_dot(hidden_two, shared_a_grad)
    shared_up_wgrad = left_dot(hidden_two, shared_b_grad)

    owned_a = matmul(rows_here, gate_here)
    owned_b = matmul(rows_here, up_here)
    owned_hidden = (jax.nn.silu(owned_a) * owned_b).astype(narrow)
    owned_up_grad = matmul(grad_here, down_here)
    owned_slot = jnp.sum(owned_up_grad * owned_hidden.astype(wide), axis=-1)
    owned_hidden_grad = weight_here[:, None] * owned_up_grad
    owned_a_grad = (owned_hidden_grad * owned_b * silu_grad(owned_a)).astype(narrow)
    owned_b_grad = (owned_hidden_grad * jax.nn.silu(owned_a)).astype(narrow)
    owned_scaled = (weight_here[:, None] * owned_hidden.astype(wide)).astype(narrow)
    owned_back = (right_dot(owned_a_grad, gate_here) + right_dot(owned_b_grad, up_here)).astype(
        narrow
    )
    back_flat = exchange(owned_back.reshape(dp_count, slot_piece, width), "dp").reshape(
        -1, width
    )
    per_slot = exchange(owned_slot.reshape(dp_count, slot_piece), "dp").reshape(1, ACTIVE, CAP)
    owned_out = (weight_here[:, None] * right_dot(owned_hidden, down_here)).astype(narrow)
    routed_flat = exchange(owned_out.reshape(dp_count, slot_piece, width), "dp").reshape(
        -1, width
    )
    terms = jnp.concatenate(
        [
            left_dot(rows_here, owned_a_grad).astype(narrow).reshape(dp_count, rows_dp, -1),
            left_dot(rows_here, owned_b_grad).astype(narrow).reshape(dp_count, rows_dp, -1),
            left_dot(grad_here, owned_scaled).astype(narrow).reshape(dp_count, rows_dp, -1),
        ],
        axis=1,
    )
    terms = exchange(terms, "dp").astype(wide)
    terms = jnp.sum(terms.reshape((ACTIVE, owner_count) + terms.shape[1:]), axis=1)
    expert_gate_grad = terms[:, :rows_dp]
    expert_up_wgrad = terms[:, rows_dp : 2 * rows_dp]
    expert_down_grad = jnp.swapaxes(terms[:, 2 * rows_dp :], 1, 2)

    hidden_two_share = hidden_two_share + matmul(pick, back_flat)
    gate_share = jnp.sum(jnp.where(places, per_slot, 0.0), axis=-1)
    gate_grad = jnp.sum(shift_blocks(gate_share), 0)
    hidden_two_grad = scatter_tensor(hidden_two_share)
    prob_own = jax.nn.softmax(matmul(hidden_two_own, router), axis=-1)
    prob_grad = jnp.concatenate(
        [gate_grad, jnp.zeros((own_rows, prob_own.shape[1] - ACTIVE), wide)], axis=-1
    )
    logit_grad = (
        prob_own * (prob_grad - jnp.sum(prob_own * prob_grad, axis=-1, keepdims=True))
    ).astype(narrow)
    router_grad = left_dot(hidden_two_own, logit_grad)
    hidden_two_grad = hidden_two_grad + right_dot(logit_grad, router)
    gain_two_grad = jnp.sum(hidden_two_grad * normed_two, axis=0)
    after_attn_grad = out_grad.astype(wide) + norm_back(
        hidden_two_grad * gain_two, normed_two, scale_two
    )
    residual_low = gather_tensor(after_attn_grad.astype(narrow))
    moe_own = scatter_tensor(moe_share + matmul(pick, routed_flat))
    block_out = (after_attn + moe_own).astype(narrow)

    mixed_grad = right_dot(residual_low, output_full).astype(narrow).reshape(group, heads, VDIM)
    output_grad = left_dot(mixed_flat, residual_low)
    query_nope_grad, query_rope_grad, key_nope_grad, key_rope_grad, values_grad = attend_backward(
        query_nope, query_rope, key_nope, key_rope, values, mixed, mixed_grad, logsum, seen
    )
    keyvalue_grad = (
        jnp.concatenate([key_nope_grad, values_grad], axis=-1)
        .astype(narrow)
        .reshape(group, heads * (NOPE + VDIM))
    )
    latent_grad = right_dot(keyvalue_grad, kv_up_full)
    gain_lat_grad = jnp.sum(latent_grad * normed_lat, axis=0)
    compressed_grad = norm_back(latent_grad * gain_lat, normed_lat, scale_lat)
    key_rope_back = unrotate(key_rope_grad, cosine, sine)
    latent_in_share = jnp.concatenate([compressed_grad, key_rope_back], axis=-1)
    latent_in_low = jnp.sum(
        shift_blocks(latent_in_share.astype(narrow)).astype(wide), axis=0
    ).astype(narrow)
    query_rope_back = unrotate(query_rope_grad, cosine[:, None, :], sine[:, None, :])
    query_grad = (
        jnp.concatenate([query_nope_grad, query_rope_back], axis=-1)
        .astype(narrow)
        .reshape(group, heads * (NOPE + ROPE))
    )
    hidden_one_share = right_dot(query_grad, query_full)
    hidden_one_grad = scatter_tensor(hidden_one_share)
    query_wgrad = left_dot(hidden_one, query_grad)
    kv_up_grad = left_dot(latent, keyvalue_grad)
    latent_back = right_dot(latent_in_low, kv_down)
    hidden_one_grad = hidden_one_grad + latent_back
    scale_one = rms_scale(residual_in)
    normed_one = residual_in * scale_one
    input_grad = after_attn_grad + norm_back(hidden_one_grad * gain_one, normed_one, scale_one)

    def by_dp(values, axis):
        shape = values.shape
        values = values.reshape(
            shape[:axis] + (dp_count, shape[axis] // dp_count) + shape[axis + 1 :]
        )
        return jnp.moveaxis(values, axis, 0).astype(narrow)

    dense_grads = (
        scatter_dp(by_dp(query_wgrad, 0), first_order),
        scatter_dp(by_dp(kv_up_grad, 0), second_order),
        scatter_dp(by_dp(output_grad, 1), second_order),
        scatter_dp(by_dp(shared_gate_grad, 0), first_order),
        scatter_dp(by_dp(shared_up_wgrad, 0), second_order),
        scatter_dp(by_dp(shared_down_grad, 1), first_order),
    )

    hidden_own = hidden_one[:own_rows]
    tall = jnp.concatenate([left_dot(hidden_own, latent_in_low), router_grad], axis=1)
    tall = tall.reshape(dp_count, tensor_count, -1, tall.shape[1])
    tall = jnp.sum(exchange(jnp.swapaxes(tall, 0, 1).astype(narrow), "tensor").astype(wide), 0)
    tall = jnp.sum(exchange(tall.astype(narrow), "dp").astype(wide), 0)
    kv_down_grad = tall[:, : LATENT + ROPE]
    router_grad = tall[:, LATENT + ROPE :]
    gain_one_grad = jnp.sum(hidden_one_share * (residual_all * scale_all), axis=0) + jnp.sum(
        latent_back * normed_one, axis=0
    )
    devices = dp_count * tensor_count
    gain_grads = jnp.concatenate(
        [
            gain_one_grad.reshape(devices, -1),
            gain_two_grad.reshape(devices, -1),
            gain_lat_grad.reshape(devices, -1),
        ],
        axis=1,
    )
    gain_grads = jnp.sum(exchange(gain_grads, both), axis=0)
    return (
        block_out,
        input_grad,
        gain_grads[:split_one],
        dense_grads[0],
        kv_down_grad,
        gain_grads[2 * split_one :],
        dense_grads[1],
        dense_grads[2],
        gain_grads[split_one : 2 * split_one],
        router_grad,
        dense_grads[3],
        dense_grads[4],
        dense_grads[5],
        expert_gate_grad,
        expert_up_wgrad,
        expert_down_grad,
    )


def solution(mesh):
    in_specs = (
        P(("dp", "tensor"), None),
        P(("dp", "tensor")),
        P("dp", "tensor"),
        P(("dp", "tensor"), None),
        P(("dp", "tensor")),
        P("dp", "tensor"),
        P("tensor", "dp"),
        P(("dp", "tensor")),
        P(("dp", "tensor"), None),
        P("dp", None),
        P("dp", "tensor"),
        P("dp", "tensor"),
        P("tensor", "dp"),
        P(None, "dp", "tensor"),
        P(None, "dp", "tensor"),
        P(None, "tensor", "dp"),
        P(("dp", "tensor"), None),
    )
    out_specs = (
        P(("dp", "tensor"), None),
        P(("dp", "tensor"), None),
        P(("dp", "tensor")),
        P("dp", "tensor"),
        P(("dp", "tensor"), None),
        P(("dp", "tensor")),
        P("dp", "tensor"),
        P("tensor", "dp"),
        P(("dp", "tensor")),
        P(("dp", "tensor"), None),
        P("dp", "tensor"),
        P("dp", "tensor"),
        P("tensor", "dp"),
        P(None, "dp", "tensor"),
        P(None, "dp", "tensor"),
        P(None, "tensor", "dp"),
    )
    return jax.shard_map(
        per_device, mesh=mesh, in_specs=in_specs, out_specs=out_specs, check_vma=False
    )
```

```python
import jax
import jax.numpy as jnp
from jax import lax
from jax.experimental import pallas as pl
from jax.experimental.pallas import tpu as pltpu
from jax.sharding import PartitionSpec as P

NOPE = 128
ROPE = 64
VDIM = 128
LATENT = 512
ACTIVE = 8
SEQ = 512
CAP = 96


LANES = 128
EPSILON = 1e-06
NEGATIVE = -1e30


def matmul(left, right):
    return jnp.dot(left, right, preferred_element_type=jnp.float32)


def left_dot(left, right):
    return lax.dot_general(
        left, right, (((0,), (0,)), ((), ())), preferred_element_type=jnp.float32
    )


def right_dot(left, right):
    return lax.dot_general(
        left, right, (((left.ndim - 1,), (1,)), ((), ())), preferred_element_type=jnp.float32
    )


def einsum32(form, left, right):
    return jnp.einsum(form, left, right, preferred_element_type=jnp.float32)


def rms_scale(values):
    return lax.rsqrt(jnp.mean(values * values, axis=-1, keepdims=True) + EPSILON)


def norm_back(grad_normed, normed, scale):
    return scale * (grad_normed - normed * jnp.mean(grad_normed * normed, axis=-1, keepdims=True))


def rope_tables(position):
    halfway = ROPE // 2
    inverse = jnp.exp(-jnp.log(10000.0) * jnp.arange(halfway).astype(jnp.float32) / halfway)
    angles = position[:, None] * inverse[None, :]
    return (jnp.cos(angles), jnp.sin(angles))


def rotate(values, cosine, sine):
    halfway = ROPE // 2
    first, second = (values[..., :halfway], values[..., halfway:])
    return jnp.concatenate(
        [first * cosine - second * sine, first * sine + second * cosine], axis=-1
    )


def unrotate(grads, cosine, sine):
    halfway = ROPE // 2
    first, second = (grads[..., :halfway], grads[..., halfway:])
    return jnp.concatenate(
        [first * cosine + second * sine, second * cosine - first * sine], axis=-1
    )


def send_tensor(values, step):
    count = lax.axis_size("tensor")
    return lax.ppermute(values, "tensor", [(i, (i + step) % count) for i in range(count)])


def pieces_of(values, parts):
    rows = values.shape[0] // parts
    return [values[i * rows : (i + 1) * rows] for i in range(parts)]


def gather_tensor(own, parts=2):
    pieces = pieces_of(own, parts)
    found = [list(pieces)]
    for _ in range(1, lax.axis_size("tensor")):
        pieces = [send_tensor(piece, -1) for piece in pieces]
        found.append(list(pieces))
    return jnp.concatenate([piece for row in found for piece in row], axis=0)


def scatter_tensor(share, parts=2):
    count = lax.axis_size("tensor")
    blocks = share.reshape((count, share.shape[0] // count) + share.shape[1:])
    sums = [piece.astype(jnp.bfloat16) for piece in pieces_of(blocks[count - 1], parts)]
    for step in range(1, count):
        sums = [send_tensor(piece.astype(jnp.bfloat16), 1) for piece in sums]
        sums = [
            piece.astype(jnp.float32) + more.astype(jnp.float32)
            for piece, more in zip(sums, pieces_of(blocks[count - 1 - step], parts))
        ]
    return jnp.concatenate(sums, axis=0)


def with_column(rows, column):
    high = column.astype(jnp.bfloat16)
    low = (column - high.astype(jnp.float32)).astype(jnp.bfloat16)
    return jnp.concatenate(
        [rows, jnp.pad(jnp.stack([high, low], axis=1), ((0, 0), (0, LANES - 2)))], axis=1
    )


def column_of(rows, place):
    return jnp.sum(rows[:, place : place + 2].astype(jnp.float32), axis=1)


def exchange(values, axes):
    return lax.all_to_all(values, axes, split_axis=0, concat_axis=0, tiled=True)


def dp_orders():
    count = lax.axis_size("dp")
    masks = [1 << k for k in range(count.bit_length() - 1)]
    return (masks[1:] + masks[:1], masks[:0:-1] + masks[:1])


def swap_dp(values, mask):
    count = lax.axis_size("dp")
    return lax.ppermute(values, "dp", [(i, i ^ mask) for i in range(count)])


def axis_of(mask):
    return lax.axis_size("dp").bit_length() - 1 - mask.bit_length()


def gather_dp(own, order):
    count = lax.axis_size("dp")
    index = lax.axis_index("dp")
    current = own.reshape((1,) * (count.bit_length() - 1) + own.shape)
    for mask in order:
        other = swap_dp(current, mask)
        high = (index & mask) > 0
        current = jnp.concatenate(
            [jnp.where(high, other, current), jnp.where(high, current, other)],
            axis=axis_of(mask),
        )
    return current.reshape((count,) + own.shape)


def scatter_dp(blocks, order):
    count = lax.axis_size("dp")
    index = lax.axis_index("dp")
    own = blocks.shape[1:]
    current = blocks.reshape((2,) * (count.bit_length() - 1) + own)
    for mask in order[::-1]:
        high = ((index & mask) > 0).astype(jnp.int32)
        axis = axis_of(mask)
        keep = lax.dynamic_slice_in_dim(current, high, 1, axis)
        give = lax.dynamic_slice_in_dim(current, 1 - high, 1, axis).astype(jnp.bfloat16)
        got = swap_dp(give, mask)
        current = keep.astype(jnp.float32) + got.astype(jnp.float32)
    return current.reshape(own)


def wide_rows(blocks):
    return jnp.moveaxis(blocks, 0, 1).reshape(blocks.shape[1], -1)


def tall_blocks(values):
    count = lax.axis_size("dp")
    values = values.reshape(values.shape[0], count, -1)
    return jnp.moveaxis(values, 1, 0).astype(jnp.bfloat16)


def causal_scores(query_nope, query_rope, key_nope, key_rope, seen):
    scores = einsum32("qhd,khd->hqk", query_nope, key_nope)
    scores = scores + einsum32("qhd,kd->hqk", query_rope, key_rope)
    return jnp.where(seen[None], scores * (NOPE + ROPE) ** (-0.5), NEGATIVE)


def attend_forward(query_nope, query_rope, key_nope, key_rope, values, seen):
    scores = causal_scores(query_nope, query_rope, key_nope, key_rope, seen)
    logsum = jax.nn.logsumexp(scores, axis=-1)
    probs = jnp.exp(scores - logsum[..., None]).astype(jnp.bfloat16)
    return (einsum32("hqk,khd->qhd", probs, values).astype(jnp.bfloat16), logsum)


def attend_backward(
    query_nope, query_rope, key_nope, key_rope, values, mixed, mixed_grad, logsum, seen
):
    scores = causal_scores(query_nope, query_rope, key_nope, key_rope, seen)
    probs_full = jnp.exp(scores - logsum[..., None])
    probs = probs_full.astype(jnp.bfloat16)
    values_grad = einsum32("hqk,qhd->khd", probs, mixed_grad)
    probs_grad = einsum32("qhd,khd->hqk", mixed_grad, values)
    delta = einsum32("qhd,qhd->hq", mixed_grad, mixed)
    score_grad = (probs_full * (probs_grad - delta[..., None]) * (NOPE + ROPE) ** (-0.5)).astype(
        jnp.bfloat16
    )
    query_nope_grad = einsum32("hqk,khd->qhd", score_grad, key_nope)
    query_rope_grad = einsum32("hqk,kd->qhd", score_grad, key_rope)
    key_nope_grad = einsum32("hqk,qhd->khd", score_grad, query_nope)
    key_rope_grad = einsum32("hqk,qhd->kd", score_grad, query_rope)
    return (query_nope_grad, query_rope_grad, key_nope_grad, key_rope_grad, values_grad)


def regroup(blocks, count):
    if blocks.shape[0] == count:
        return blocks
    values = jnp.moveaxis(blocks, 0, 1).reshape(blocks.shape[1], count, -1)
    return jnp.moveaxis(values, 1, 0)


def lane_count(blocks):
    return min(blocks.shape[0], blocks.shape[0] * blocks.shape[2] // LANES)


def dot_of(left, right, dims):
    return lax.dot_general(left, right, ((dims[:1], dims[1:]), ((), ())), preferred_element_type=jnp.float32)


def swiglu_parts(first, second, grad):
    sigma = 1.0 / (1.0 + jnp.exp(-first))
    gated = first * sigma
    return (gated * second, grad * second * (sigma * (1.0 + first * (1.0 - sigma))), grad * gated)


def call_kernel(body, outs, scratch, *arguments):
    return pl.pallas_call(
        body,
        out_shape=[jax.ShapeDtypeStruct(shape, dtype) for shape, dtype in outs],
        scratch_shapes=[pltpu.VMEM(shape, dtype) for shape, dtype in scratch],
    )(*arguments)


def shared_experts(hidden, grad, first, second, units):
    narrow = jnp.bfloat16
    rows, width = hidden.shape
    given = first.shape[0]
    first, second = [regroup(blocks, lane_count(blocks)) for blocks in (first, second)]
    count, _, part = first.shape
    half = units // 2

    def body(x_ref, g_ref, first_ref, second_ref, out_ref, back_ref, dfirst_ref, dsecond_ref,
             gate_ref, up_ref, down_ref):
        for j in range(count):
            lanes = slice(j * part, (j + 1) * part)
            gate_ref[:, lanes] = first_ref[j, :units]
            up_ref[:, lanes] = second_ref[j, :units]
            down_ref[:half, lanes] = first_ref[j, units:]
            down_ref[half:, lanes] = second_ref[j, units:]
        a = dot_of(x_ref[...], gate_ref[...], (1, 1))
        b = dot_of(x_ref[...], up_ref[...], (1, 1))
        u = dot_of(g_ref[...], down_ref[...], (1, 1))
        h, da, db = [v.astype(narrow) for v in swiglu_parts(a, b, u)]
        out_ref[...] = dot_of(h, down_ref[...], (1, 0)).astype(narrow)
        back_ref[...] = dot_of(da, gate_ref[...], (1, 0)) + dot_of(db, up_ref[...], (1, 0))
        dgate = dot_of(da, x_ref[...], (0, 0)).astype(narrow)
        dup = dot_of(db, x_ref[...], (0, 0)).astype(narrow)
        ddown = dot_of(h, g_ref[...], (0, 0)).astype(narrow)
        for j in range(count):
            lanes = slice(j * part, (j + 1) * part)
            dfirst_ref[j, :units] = dgate[:, lanes]
            dsecond_ref[j, :units] = dup[:, lanes]
            dfirst_ref[j, units:] = ddown[:half, lanes]
            dsecond_ref[j, units:] = ddown[half:, lanes]

    wide_scratch = ((units, width), narrow)
    out, back, dfirst, dsecond = call_kernel(
        body,
        [((rows, width), narrow), ((rows, width), jnp.float32), (first.shape, narrow), (second.shape, narrow)],
        [wide_scratch] * 3,
        hidden, grad, first, second,
    )
    return out, back, regroup(dfirst, given), regroup(dsecond, given)


def load_slab(slab_ref, wide_ref, place, units):
    part = slab_ref.shape[2]
    for j in range(slab_ref.shape[0]):
        wide_ref[:, j * part : (j + 1) * part] = slab_ref[j, place * units : (place + 1) * units]


def owned_first(rows, grads, slabs):
    narrow = jnp.bfloat16
    slots, width = grads.shape
    units = slabs.shape[1] // 3
    slabs = regroup(slabs, lane_count(slabs))

    def body(x_ref, g_ref, slab_ref, back_ref, da_ref, db_ref, scaled_ref, gate_ref, up_ref, down_ref):
        load_slab(slab_ref, gate_ref, 0, units)
        load_slab(slab_ref, up_ref, 1, units)
        load_slab(slab_ref, down_ref, 2, units)
        x = x_ref[:, :width]
        extra = x_ref[:, width:].astype(jnp.float32)
        weight = extra[:, 0:1] + extra[:, 1:2]
        a = dot_of(x, gate_ref[...], (1, 1))
        b = dot_of(x, up_ref[...], (1, 1))
        u = dot_of(g_ref[...], down_ref[...], (1, 1))
        h, da, db = swiglu_parts(a, b, u)
        h = h.astype(narrow).astype(jnp.float32)
        slot = jnp.sum(u * h, axis=1, keepdims=True)
        da = (weight * da).astype(narrow)
        db = (weight * db).astype(narrow)
        da_ref[...] = da
        db_ref[...] = db
        scaled_ref[...] = (weight * h).astype(narrow)
        back_ref[:, :width] = (
            dot_of(da, gate_ref[...], (1, 0)) + dot_of(db, up_ref[...], (1, 0))
        ).astype(narrow)
        lane = lax.broadcasted_iota(jnp.int32, (slots, LANES), 1)
        high = slot.astype(narrow).astype(jnp.float32)
        column = jnp.where(lane == 0, high, jnp.where(lane == 1, slot - high, 0.0))
        back_ref[:, width:] = column.astype(narrow)

    inner = ((slots, units), narrow)
    return call_kernel(
        body, [(rows.shape, narrow), inner, inner, inner], [((units, width), narrow)] * 3,
        rows, grads, slabs,
    )


def owned_second(rows, grads, slabs, da, db, scaled):
    narrow = jnp.bfloat16
    slots, width = grads.shape
    units = slabs.shape[1] // 3
    given = slabs.shape[0]
    slabs = regroup(slabs, lane_count(slabs))

    def body(x_ref, g_ref, slab_ref, da_ref, db_ref, scaled_ref, out_ref, term_ref, down_ref):
        part = slab_ref.shape[2]
        load_slab(slab_ref, down_ref, 2, units)
        out_ref[...] = dot_of(scaled_ref[...], down_ref[...], (1, 0)).astype(narrow)
        x = x_ref[:, :width]
        for place, value in enumerate(
            (dot_of(da_ref[...], x, (0, 0)), dot_of(db_ref[...], x, (0, 0)),
             dot_of(scaled_ref[...], g_ref[...], (0, 0)))
        ):
            for j in range(slab_ref.shape[0]):
                term_ref[j, place * units : (place + 1) * units] = value[
                    :, j * part : (j + 1) * part
                ].astype(narrow)

    out, terms = call_kernel(
        body, [((slots, width), narrow), (slabs.shape, narrow)], [((units, width), narrow)],
        rows, grads, slabs, da, db, scaled,
    )
    return out, regroup(terms, given)


def block(
    block_in,
    attn_norm_gain,
    query_weight,
    kv_down_weight,
    latent_gain,
    kv_up_weight,
    output_weight,
    ffn_norm_gain,
    router_weight,
    expert_ids,
    shared_gate_weight,
    shared_up_weight,
    shared_down_weight,
    expert_gate_weight,
    expert_up_weight,
    expert_down_weight,
    out_grad,
):
    wide = jnp.float32
    narrow = jnp.bfloat16
    own_rows = block_in.shape[0]
    width = block_in.shape[1]
    dp_count = lax.axis_size("dp")
    tensor_count = lax.axis_size("tensor")
    tensor_index = lax.axis_index("tensor")
    group = own_rows * tensor_count
    owner_count = dp_count // ACTIVE
    slot_piece = CAP // owner_count
    slots = ACTIVE * CAP
    both = ("dp", "tensor")
    first_order, second_order = dp_orders()

    all_in = gather_tensor(block_in)
    small = jnp.concatenate([kv_down_weight, router_weight], axis=1)
    small = exchange(jnp.broadcast_to(small[None], (tensor_count,) + small.shape), "tensor")
    gains = jnp.concatenate([attn_norm_gain, ffn_norm_gain, latent_gain])
    gains = exchange(
        jnp.broadcast_to(gains[None], (dp_count * tensor_count, gains.shape[0])), both
    ).astype(wide)
    split_one = attn_norm_gain.shape[0]
    gain_one = gains[:, :split_one].reshape(-1)
    gain_two = gains[:, split_one : 2 * split_one].reshape(-1)
    gain_lat = gains[:, 2 * split_one :].reshape(-1)

    query_full = gather_dp(query_weight, first_order).reshape(width, -1)
    small = gather_dp(small, second_order).reshape(width, -1)
    kv_up_full = gather_dp(kv_up_weight, second_order).reshape(LATENT, -1)
    kv_down = small[:, : LATENT + ROPE]
    router = small[:, LATENT + ROPE :]
    output_full = wide_rows(gather_dp(output_weight, second_order))
    grad_all = gather_tensor(out_grad, 1)

    shared_units = shared_down_weight.shape[0]
    half = shared_units // 2
    shared = (
        gather_dp(jnp.concatenate([shared_gate_weight.T, shared_down_weight[:half]]), first_order),
        gather_dp(jnp.concatenate([shared_up_weight.T, shared_down_weight[half:]]), second_order),
    )
    units = expert_down_weight.shape[1]
    slabs = jnp.concatenate(
        [
            jnp.swapaxes(expert_gate_weight, 1, 2),
            jnp.swapaxes(expert_up_weight, 1, 2),
            expert_down_weight,
        ],
        axis=1,
    )
    slabs = exchange(jnp.repeat(slabs, owner_count, axis=0), "dp")

    heads = query_full.shape[1] // (NOPE + ROPE)
    residual_all = all_in.astype(wide)
    scale_all = rms_scale(residual_all)
    hidden_one = (residual_all * scale_all * gain_one).astype(narrow)
    latent_in = matmul(hidden_one, kv_down).astype(narrow)
    compressed = latent_in[:, :LATENT].astype(wide)
    scale_lat = rms_scale(compressed)
    normed_lat = compressed * scale_lat
    latent = (normed_lat * gain_lat).astype(narrow)
    place = (jnp.arange(group) + tensor_index * own_rows) % group
    position = (place % SEQ).astype(wide)
    sequence = place // SEQ
    seen = (place[:, None] >= place[None, :]) & (sequence[:, None] == sequence[None, :])
    cosine, sine = rope_tables(position)
    key_rope = rotate(latent_in[:, LATENT:].astype(wide), cosine, sine).astype(narrow)
    query = matmul(hidden_one, query_full).reshape(group, heads, NOPE + ROPE)
    query_nope = query[..., :NOPE].astype(narrow)
    query_rope = rotate(query[..., NOPE:], cosine[:, None, :], sine[:, None, :]).astype(narrow)
    keyvalue = matmul(latent, kv_up_full).astype(narrow).reshape(group, heads, NOPE + VDIM)
    key_nope = keyvalue[..., :NOPE]
    values = keyvalue[..., NOPE:]
    mixed, logsum = attend_forward(query_nope, query_rope, key_nope, key_rope, values, seen)
    mixed_flat = mixed.reshape(group, heads * VDIM)
    attn_share = matmul(mixed_flat, output_full)
    attn_own = scatter_tensor(attn_share)

    residual_in = block_in.astype(wide)
    after_attn = residual_in + attn_own
    scale_two = rms_scale(after_attn)
    normed_two = after_attn * scale_two
    hidden_two_own = (normed_two * gain_two).astype(narrow)
    hidden_two = gather_tensor(hidden_two_own)

    ids = jnp.concatenate([expert_ids, expert_ids], axis=0)
    ids = lax.dynamic_slice_in_dim(ids, tensor_index * own_rows, group, 0)
    chosen = jnp.any(ids[:, :, None] == jnp.arange(ACTIVE, dtype=jnp.int32)[None, None, :], axis=1)
    ranks = jnp.cumsum(chosen.astype(jnp.int32), axis=0) - 1
    places = (ranks[:, :, None] == jnp.arange(CAP, dtype=jnp.int32)[None, None, :]) & chosen[
        :, :, None
    ]
    pick = places.astype(narrow).reshape(group, slots)
    grad_in = left_dot(pick, grad_all).astype(narrow)
    grad_here = exchange(grad_in.reshape(dp_count, slot_piece, width), "dp").reshape(-1, width)
    route_prob = jax.nn.softmax(matmul(hidden_two, router), axis=-1)
    gate = jnp.where(chosen, route_prob[:, :ACTIVE], 0.0)
    weight = jnp.sum(jnp.where(places, gate[:, :, None], 0.0), axis=0).reshape(slots)
    tokens_in = with_column(left_dot(pick, hidden_two).astype(narrow), weight)
    rows_here = exchange(tokens_in.reshape(dp_count, slot_piece, -1), "dp")
    rows_here = rows_here.reshape(slots, -1)

    moe_share, hidden_two_share, shared_first, shared_second = shared_experts(
            hidden_two, grad_all, shared[0], shared[1], shared_units
    )

    owned_back, owned_a_grad, owned_b_grad, owned_scaled = owned_first(rows_here, grad_here, slabs)
    back_flat = exchange(owned_back.reshape(dp_count, slot_piece, -1), "dp")
    back_flat = back_flat.reshape(slots, -1)
    per_slot = column_of(back_flat, width).reshape(1, ACTIVE, CAP)
    back_flat = back_flat[:, :width]
    owned_out, terms = owned_second(
            rows_here, grad_here, slabs, owned_a_grad, owned_b_grad, owned_scaled
    )
    routed_flat = exchange(owned_out.reshape(dp_count, slot_piece, width), "dp").reshape(-1, width)
    terms = exchange(terms, "dp")
    terms = terms.reshape((ACTIVE, owner_count) + terms.shape[1:])

    def summed(first):
        return jnp.sum(terms[:, :, first : first + units].astype(wide), axis=1)

    expert_gate_grad = jnp.swapaxes(summed(0), 1, 2)
    expert_up_wgrad = jnp.swapaxes(summed(units), 1, 2)
    expert_down_grad = summed(2 * units)

    hidden_two_share = hidden_two_share + matmul(pick, back_flat)
    gate_share = jnp.sum(jnp.where(places, per_slot, 0.0), axis=-1)
    hidden_two_share = jnp.concatenate(
            [hidden_two_share, jnp.pad(gate_share, ((0, 0), (0, LANES - ACTIVE)))], axis=1
    )
    hidden_two_grad = scatter_tensor(hidden_two_share)
    gate_grad = hidden_two_grad[:, width : width + ACTIVE]
    hidden_two_grad = hidden_two_grad[:, :width]
    prob_own = jax.nn.softmax(matmul(hidden_two_own, router), axis=-1)
    prob_grad = jnp.concatenate(
        [gate_grad, jnp.zeros((own_rows, prob_own.shape[1] - ACTIVE), wide)], axis=-1
    )
    logit_grad = (
        prob_own * (prob_grad - jnp.sum(prob_own * prob_grad, axis=-1, keepdims=True))
    ).astype(narrow)
    router_grad = left_dot(hidden_two_own, logit_grad)
    hidden_two_grad = hidden_two_grad + right_dot(logit_grad, router)
    gain_two_grad = jnp.sum(hidden_two_grad * normed_two, axis=0)
    after_attn_grad = out_grad.astype(wide) + norm_back(
            hidden_two_grad * gain_two, normed_two, scale_two
    )
    residual_low = gather_tensor(after_attn_grad.astype(narrow))
    moe_share = moe_share.astype(wide) + matmul(pick, routed_flat)
    moe_own = scatter_tensor(moe_share, 1)
    block_out = (after_attn + moe_own).astype(narrow)

    mixed_grad = right_dot(residual_low, output_full).astype(narrow).reshape(group, heads, VDIM)
    output_grad = left_dot(mixed_flat, residual_low)
    query_nope_grad, query_rope_grad, key_nope_grad, key_rope_grad, values_grad = attend_backward(
            query_nope, query_rope, key_nope, key_rope, values, mixed, mixed_grad, logsum, seen
    )
    keyvalue_grad = (
        jnp.concatenate([key_nope_grad, values_grad], axis=-1)
        .astype(narrow)
        .reshape(group, heads * (NOPE + VDIM))
    )
    latent_grad = right_dot(keyvalue_grad, kv_up_full)
    gain_lat_grad = jnp.sum(latent_grad * normed_lat, axis=0)
    compressed_grad = norm_back(latent_grad * gain_lat, normed_lat, scale_lat)
    key_rope_back = unrotate(key_rope_grad, cosine, sine)
    latent_in_share = jnp.concatenate([compressed_grad, key_rope_back], axis=-1)
    latent_in_low = latent_in_share.astype(narrow)
    query_rope_back = unrotate(query_rope_grad, cosine[:, None, :], sine[:, None, :])
    query_grad = (
        jnp.concatenate([query_nope_grad, query_rope_back], axis=-1)
        .astype(narrow)
        .reshape(group, heads * (NOPE + ROPE))
    )
    hidden_one_share = right_dot(query_grad, query_full) + right_dot(latent_in_low, kv_down)
    hidden_one_grad = scatter_tensor(hidden_one_share)
    query_wgrad = left_dot(hidden_one, query_grad)
    kv_up_grad = left_dot(latent, keyvalue_grad)
    scale_one = rms_scale(residual_in)
    normed_one = residual_in * scale_one
    input_grad = after_attn_grad + norm_back(hidden_one_grad * gain_one, normed_one, scale_one)

    tall = jnp.concatenate(
        [left_dot(hidden_one, latent_in_low), router_grad], axis=1
    ).astype(narrow)
    tall = tall.reshape(dp_count, -1, tall.shape[1])
    shared_first = scatter_dp(shared_first, first_order)
    shared_second = scatter_dp(shared_second, second_order)
    shared_grads = (
        shared_first[:shared_units].T,
        shared_second[:shared_units].T,
        jnp.concatenate([shared_first[shared_units:], shared_second[shared_units:]]),
    )
    output_grad = scatter_dp(tall_blocks(output_grad), second_order)
    query_wgrad = query_wgrad.astype(narrow).reshape(dp_count, -1, query_wgrad.shape[1])
    query_wgrad = scatter_dp(query_wgrad, first_order)
    kv_up_grad = kv_up_grad.astype(narrow).reshape(dp_count, -1, kv_up_grad.shape[1])
    kv_up_grad = scatter_dp(kv_up_grad, second_order)
    tall = scatter_dp(tall, second_order).astype(narrow)
    tall = exchange(tall.reshape(tensor_count, -1, tall.shape[1]), "tensor")
    tall = jnp.sum(tall.astype(wide), axis=0)
    kv_down_grad = tall[:, : LATENT + ROPE]
    router_grad = tall[:, LATENT + ROPE :]
    gain_one_grad = jnp.sum(hidden_one_share * (residual_all * scale_all), axis=0)
    devices = dp_count * tensor_count
    gain_grads = jnp.concatenate(
        [
            gain_one_grad.reshape(devices, -1),
            gain_two_grad.reshape(devices, -1),
            gain_lat_grad.reshape(devices, -1),
        ],
        axis=1,
    )
    gain_grads = jnp.sum(exchange(gain_grads, both), axis=0)
    return (
        block_out,
        input_grad,
        gain_grads[:split_one],
        query_wgrad,
        kv_down_grad,
        gain_grads[2 * split_one :],
        kv_up_grad,
        output_grad,
        gain_grads[split_one : 2 * split_one],
        router_grad,
        shared_grads[0],
        shared_grads[1],
        shared_grads[2],
        expert_gate_grad,
        expert_up_wgrad,
        expert_down_grad,
    )


def solution(mesh):
    in_specs = (
        P(("dp", "tensor"), None),
        P(("dp", "tensor")),
        P("dp", "tensor"),
        P(("dp", "tensor"), None),
        P(("dp", "tensor")),
        P("dp", "tensor"),
        P("tensor", "dp"),
        P(("dp", "tensor")),
        P(("dp", "tensor"), None),
        P("dp", None),
        P("dp", "tensor"),
        P("dp", "tensor"),
        P("tensor", "dp"),
        P(None, "dp", "tensor"),
        P(None, "dp", "tensor"),
        P(None, "tensor", "dp"),
        P(("dp", "tensor"), None),
    )
    out_specs = (
        P(("dp", "tensor"), None),
        P(("dp", "tensor"), None),
        P(("dp", "tensor")),
        P("dp", "tensor"),
        P(("dp", "tensor"), None),
        P(("dp", "tensor")),
        P("dp", "tensor"),
        P("tensor", "dp"),
        P(("dp", "tensor")),
        P(("dp", "tensor"), None),
        P("dp", "tensor"),
        P("dp", "tensor"),
        P("tensor", "dp"),
        P(None, "dp", "tensor"),
        P(None, "dp", "tensor"),
        P(None, "tensor", "dp"),
    )
    return jax.shard_map(block, mesh=mesh, in_specs=in_specs, out_specs=out_specs, check_vma=False)
```

```python
import jax
import jax.numpy as jnp
from jax import lax
from jax.experimental import pallas as pl
from jax.experimental.pallas import tpu as pltpu
from jax.sharding import PartitionSpec as P

NOPE = 128
ROPE = 64
VDIM = 128
LATENT = 512
ACTIVE = 8
SEQ = 512
CAP = 96


LANES = 128
DP = "dp"
TENSOR = "tensor"
EPSILON = 1e-06
NEGATIVE = -1e30


def matmul(left, right):
    return jnp.dot(left, right, preferred_element_type=jnp.float32)


def left_dot(left, right):
    return lax.dot_general(
        left, right, (((0,), (0,)), ((), ())), preferred_element_type=jnp.float32
    )


def right_dot(left, right):
    return lax.dot_general(
        left, right, (((left.ndim - 1,), (1,)), ((), ())), preferred_element_type=jnp.float32
    )


def einsum32(form, left, right):
    return jnp.einsum(form, left, right, preferred_element_type=jnp.float32)


def rms_scale(values):
    return lax.rsqrt(jnp.mean(values * values, axis=-1, keepdims=True) + EPSILON)


def norm_back(grad_normed, normed, scale):
    return scale * (grad_normed - normed * jnp.mean(grad_normed * normed, axis=-1, keepdims=True))


def rope_tables(position):
    halfway = ROPE // 2
    inverse = jnp.exp(-jnp.log(10000.0) * jnp.arange(halfway).astype(jnp.float32) / halfway)
    angles = position[:, None] * inverse[None, :]
    return (jnp.cos(angles), jnp.sin(angles))


def rotate(values, cosine, sine):
    halfway = ROPE // 2
    first, second = (values[..., :halfway], values[..., halfway:])
    return jnp.concatenate(
        [first * cosine - second * sine, first * sine + second * cosine], axis=-1
    )


def unrotate(grads, cosine, sine):
    halfway = ROPE // 2
    first, second = (grads[..., :halfway], grads[..., halfway:])
    return jnp.concatenate(
        [first * cosine + second * sine, second * cosine - first * sine], axis=-1
    )


def send_tensor(values, step):
    count = lax.axis_size(TENSOR)
    return lax.ppermute(values, TENSOR, [(i, (i + step) % count) for i in range(count)])


def pieces_of(values, parts):
    rows = values.shape[0] // parts
    return [values[i * rows : (i + 1) * rows] for i in range(parts)]


def gather_tensor(own, parts=2):
    pieces = pieces_of(own, parts)
    found = list(pieces)
    for _ in range(1, lax.axis_size(TENSOR)):
        pieces = [send_tensor(piece, -1) for piece in pieces]
        found += pieces
    return found


def scatter_tensor(share, parts=2):
    count = lax.axis_size(TENSOR)
    blocks = share.reshape((count, share.shape[0] // count) + share.shape[1:])
    sums = [piece.astype(jnp.bfloat16) for piece in pieces_of(blocks[count - 1], parts)]
    for step in range(1, count):
        sums = [send_tensor(piece, 1) for piece in sums]
        sums = [
            piece.astype(jnp.float32) + more.astype(jnp.float32)
            for piece, more in zip(sums, pieces_of(blocks[count - 1 - step], parts))
        ]
        if step < count - 1:
            sums = [piece.astype(jnp.bfloat16) for piece in sums]
    return jnp.concatenate(sums, axis=0)


def exchange(values, axes):
    return lax.all_to_all(values, axes, split_axis=0, concat_axis=0, tiled=True)


def dp_orders():
    count = lax.axis_size(DP)
    masks = [1 << k for k in range(count.bit_length() - 1)]
    return (masks[1:] + masks[:1], masks[:0:-1] + masks[:1])


def swap_dp(values, mask):
    count = lax.axis_size(DP)
    return lax.ppermute(values, DP, [(i, i ^ mask) for i in range(count)])


def axis_of(mask):
    return lax.axis_size(DP).bit_length() - 1 - mask.bit_length()


def gather_dp(own, order, apart=False):
    count = lax.axis_size(DP)
    index = lax.axis_index(DP)
    current = own.reshape((1,) * (count.bit_length() - 1) + own.shape)
    for step, mask in enumerate(order):
        other = swap_dp(current, mask)
        if apart and step + 1 == len(order):
            return [values.reshape((count // 2,) + own.shape) for values in (current, other)]
        high = (index & mask) > 0
        current = jnp.concatenate(
            [jnp.where(high, other, current), jnp.where(high, current, other)],
            axis=axis_of(mask),
        )
    return current.reshape((count,) + own.shape)


def scatter_dp(blocks, order):
    count = lax.axis_size(DP)
    index = lax.axis_index(DP)
    bits = count.bit_length() - 1
    pair = isinstance(blocks, (tuple, list))
    own = blocks[0].shape[1:] if pair else blocks.shape[1:]
    current = None if pair else blocks.reshape((2,) * bits + own)
    for mask in order[::-1]:
        high = ((index & mask) > 0).astype(jnp.int32)
        axis = axis_of(mask)
        if current is None:
            keep, give = [half.reshape((2,) * (bits - 1) + (1,) + own) for half in blocks]
        else:
            keep = lax.dynamic_slice_in_dim(current, high, 1, axis)
            give = lax.dynamic_slice_in_dim(current, 1 - high, 1, axis).astype(jnp.bfloat16)
        got = swap_dp(give, mask)
        current = keep.astype(jnp.float32) + got.astype(jnp.float32)
    return current.reshape(own)


def wide_rows(blocks):
    return jnp.moveaxis(blocks, 0, 1).reshape(blocks.shape[1], -1)


def tall_blocks(values):
    count = lax.axis_size(DP)
    values = values.reshape(values.shape[0], count, -1)
    return jnp.moveaxis(values, 1, 0).astype(jnp.bfloat16)


def causal_scores(query_nope, query_rope, key_nope, key_rope, seen):
    scores = einsum32("qhd,khd->hqk", query_nope, key_nope)
    scores = scores + einsum32("qhd,kd->hqk", query_rope, key_rope)
    return jnp.where(seen[None], scores * (NOPE + ROPE) ** (-0.5), NEGATIVE)


def attend_forward(query_nope, query_rope, key_nope, key_rope, values, seen):
    scores = causal_scores(query_nope, query_rope, key_nope, key_rope, seen)
    logsum = jax.nn.logsumexp(scores, axis=-1)
    probs = jnp.exp(scores - logsum[..., None]).astype(jnp.bfloat16)
    return (einsum32("hqk,khd->qhd", probs, values).astype(jnp.bfloat16), logsum)


def attend_backward(
    query_nope, query_rope, key_nope, key_rope, values, mixed, mixed_grad, logsum, seen
):
    scores = causal_scores(query_nope, query_rope, key_nope, key_rope, seen)
    probs_full = jnp.exp(scores - logsum[..., None])
    probs = probs_full.astype(jnp.bfloat16)
    values_grad = einsum32("hqk,qhd->khd", probs, mixed_grad)
    probs_grad = einsum32("qhd,khd->hqk", mixed_grad, values)
    delta = einsum32("qhd,qhd->hq", mixed_grad, mixed)
    score_grad = (probs_full * (probs_grad - delta[..., None]) * (NOPE + ROPE) ** (-0.5)).astype(
        jnp.bfloat16
    )
    query_nope_grad = einsum32("hqk,khd->qhd", score_grad, key_nope)
    query_rope_grad = einsum32("hqk,kd->qhd", score_grad, key_rope)
    key_nope_grad = einsum32("hqk,qhd->khd", score_grad, query_nope)
    key_rope_grad = einsum32("hqk,qhd->kd", score_grad, query_rope)
    return (query_nope_grad, query_rope_grad, key_nope_grad, key_rope_grad, values_grad)


def regroup(blocks, count):
    if blocks.shape[0] == count:
        return blocks
    values = jnp.moveaxis(blocks, 0, 1).reshape(blocks.shape[1], count, -1)
    return jnp.moveaxis(values, 1, 0)


def lane_count(blocks):
    return min(blocks.shape[0], blocks.shape[0] * blocks.shape[2] // LANES)


def dot_of(left, right, dims):
    return lax.dot_general(left, right, ((dims[:1], dims[1:]), ((), ())), preferred_element_type=jnp.float32)


def swiglu_parts(first, second, grad):
    sigma = 1.0 / (1.0 + jnp.exp(-first))
    gated = first * sigma
    return (gated * second, grad * second * (sigma * (1.0 + first * (1.0 - sigma))), grad * gated)


def call_kernel(body, outs, scratch, *arguments):
    return pl.pallas_call(
        body,
        out_shape=[jax.ShapeDtypeStruct(shape, dtype) for shape, dtype in outs],
        scratch_shapes=[pltpu.VMEM(shape, dtype) for shape, dtype in scratch],
    )(*arguments)


def mingle(pair, bit):
    mine, theirs = pair
    blocks = [jnp.where(bit > 0, theirs, mine), jnp.where(bit > 0, mine, theirs)]
    return jnp.stack(blocks, axis=1).reshape((-1,) + mine.shape[1:])


def part_by(blocks, bit):
    even, odd = blocks[0::2], blocks[1::2]
    return [jnp.where(bit > 0, odd, even), jnp.where(bit > 0, even, odd)]


def shared_experts(hidden, grad, firsts, seconds, units, bit):
    if firsts[0].shape[2] % LANES == 0:
        return shared_kernel(hidden, grad, firsts, seconds, units, bit)
    first, second = [mingle(pair, bit) for pair in (firsts, seconds)]
    given, count = first.shape[0], lane_count(first)
    pairs = [part_by(regroup(blocks, count), 0) for blocks in (first, second)]
    out, back, *pairs = shared_kernel(hidden, grad, *pairs, units, jnp.int32(0))
    pairs = [part_by(regroup(mingle(pair, 0), given), bit) for pair in pairs]
    return out, back, *pairs


def shared_kernel(hidden, grad, firsts, seconds, units, bit):
    narrow = jnp.bfloat16
    rows, width = hidden.shape
    count, _, part = firsts[0].shape
    half = units // 2

    def body(bit_ref, x_ref, g_ref, *refs):
        pairs, (out_ref, back_ref), results = refs[:4], refs[4:6], refs[6:10]
        gate_ref, up_ref, down_ref = refs[10:]
        mine = bit_ref[0]
        for j in range(count):
            for place in range(2):
                own = mine if place == 0 else 1 - mine
                lanes = pl.ds(pl.multiple_of((2 * j + own) * part, LANES), part)
                gate_ref[:, lanes] = pairs[place][j, :units]
                up_ref[:, lanes] = pairs[2 + place][j, :units]
                down_ref[:half, lanes] = pairs[place][j, units:]
                down_ref[half:, lanes] = pairs[2 + place][j, units:]
        a = dot_of(x_ref[...], gate_ref[...], (1, 1))
        b = dot_of(x_ref[...], up_ref[...], (1, 1))
        u = dot_of(g_ref[...], down_ref[...], (1, 1))
        h, da, db = [v.astype(narrow) for v in swiglu_parts(a, b, u)]
        out_ref[...] = dot_of(h, down_ref[...], (1, 0)).astype(narrow)
        back_ref[...] = dot_of(da, gate_ref[...], (1, 0)) + dot_of(db, up_ref[...], (1, 0))
        gate_ref[...] = dot_of(da, x_ref[...], (0, 0)).astype(narrow)
        up_ref[...] = dot_of(db, x_ref[...], (0, 0)).astype(narrow)
        down_ref[...] = dot_of(h, g_ref[...], (0, 0)).astype(narrow)
        for j in range(count):
            for place in range(2):
                own = mine if place == 0 else 1 - mine
                lanes = pl.ds(pl.multiple_of((2 * j + own) * part, LANES), part)
                results[place][j, :units] = gate_ref[:, lanes]
                results[2 + place][j, :units] = up_ref[:, lanes]
                results[place][j, units:] = down_ref[:half, lanes]
                results[2 + place][j, units:] = down_ref[half:, lanes]

    blocks = (firsts[0].shape, narrow)
    vmem = pl.BlockSpec(memory_space=pltpu.VMEM)
    out, back, *results = pl.pallas_call(
        body,
        in_specs=[pl.BlockSpec(memory_space=pltpu.SMEM)] + [vmem] * 6,
        out_shape=[
            jax.ShapeDtypeStruct(shape, dtype)
            for shape, dtype in [((rows, width), narrow), ((rows, width), jnp.float32)] + [blocks] * 4
        ],
        scratch_shapes=[pltpu.VMEM((units, width), narrow)] * 3,
    )(bit.reshape(1), hidden, grad, *firsts, *seconds)
    return out, back, results[:2], results[2:]


def load_slab(slab_ref, wide_ref, place, units):
    part = slab_ref.shape[2]
    for j in range(slab_ref.shape[0]):
        wide_ref[:, j * part : (j + 1) * part] = slab_ref[j, place * units : (place + 1) * units]


def owned_first(rows, grads, slabs):
    narrow = jnp.bfloat16
    slots, width = grads.shape
    units = slabs.shape[1] // 3
    slabs = regroup(slabs, lane_count(slabs))

    def body(x_ref, g_ref, slab_ref, back_ref, da_ref, db_ref, scaled_ref, gate_ref, up_ref, down_ref):
        load_slab(slab_ref, gate_ref, 0, units)
        load_slab(slab_ref, up_ref, 1, units)
        load_slab(slab_ref, down_ref, 2, units)
        x = x_ref[:, :width]
        extra = x_ref[:, width:].astype(jnp.float32)
        weight = extra[:, 0:1] + extra[:, 1:2]
        a = dot_of(x, gate_ref[...], (1, 1))
        b = dot_of(x, up_ref[...], (1, 1))
        u = dot_of(g_ref[...], down_ref[...], (1, 1))
        h, da, db = swiglu_parts(a, b, u)
        h = h.astype(narrow).astype(jnp.float32)
        slot = jnp.sum(u * h, axis=1, keepdims=True)
        da = (weight * da).astype(narrow)
        db = (weight * db).astype(narrow)
        da_ref[...] = da
        db_ref[...] = db
        scaled_ref[...] = (weight * h).astype(narrow)
        back_ref[:, :width] = (
            dot_of(da, gate_ref[...], (1, 0)) + dot_of(db, up_ref[...], (1, 0))
        ).astype(narrow)
        high = slot.astype(narrow).astype(jnp.float32)
        back_ref[:, width:] = two_lanes(high, slot - high)

    inner = ((slots, units), narrow)
    return call_kernel(
        body, [(rows.shape, narrow), inner, inner, inner], [((units, width), narrow)] * 3,
        rows, grads, slabs,
    )


def owned_second(rows, grads, slabs, da, db, scaled):
    narrow = jnp.bfloat16
    slots, width = grads.shape
    units = slabs.shape[1] // 3
    given = slabs.shape[0]
    slabs = regroup(slabs, lane_count(slabs))

    def body(x_ref, g_ref, slab_ref, da_ref, db_ref, scaled_ref, out_ref, term_ref, down_ref):
        part = slab_ref.shape[2]
        load_slab(slab_ref, down_ref, 2, units)
        out_ref[...] = dot_of(scaled_ref[...], down_ref[...], (1, 0)).astype(narrow)
        x = x_ref[:, :width]
        for place, value in enumerate(
            (dot_of(da_ref[...], x, (0, 0)), dot_of(db_ref[...], x, (0, 0)),
             dot_of(scaled_ref[...], g_ref[...], (0, 0)))
        ):
            for j in range(slab_ref.shape[0]):
                term_ref[j, place * units : (place + 1) * units] = value[
                    :, j * part : (j + 1) * part
                ].astype(narrow)

    out, terms = call_kernel(
        body, [((slots, width), narrow), (slabs.shape, narrow)], [((units, width), narrow)],
        rows, grads, slabs, da, db, scaled,
    )
    return out, regroup(terms, given)


def assemble(refs, whole_ref):
    rows = refs[0].shape[0]
    for i, ref in enumerate(refs):
        whole_ref[i * rows : (i + 1) * rows] = ref[...]


def joined(pieces):
    def body(*refs):
        assemble(refs[:-1], refs[-1])

    shape = (len(pieces) * pieces[0].shape[0], pieces[0].shape[1])
    return call_kernel(body, [(shape, pieces[0].dtype)], [], *pieces)[0]


def normed_rows(pieces, gain):
    def body(*refs):
        gain_ref, whole_ref, hidden_ref = refs[-3:]
        rows = refs[0].shape[0]
        for i, ref in enumerate(refs[:-3]):
            values = ref[...]
            whole_ref[i * rows : (i + 1) * rows] = values
            values = values.astype(jnp.float32)
            hidden_ref[i * rows : (i + 1) * rows] = (
                values * rms_scale(values) * gain_ref[...]
            ).astype(jnp.bfloat16)

    shape = (len(pieces) * pieces[0].shape[0], pieces[0].shape[1])
    return call_kernel(body, [(shape, jnp.bfloat16)] * 2, [], *pieces, gain[None])


def picked_rows(pieces, pick):
    def body(*refs):
        pick_ref, whole_ref, rows_ref = refs[-3:]
        assemble(refs[:-3], whole_ref)
        rows_ref[...] = dot_of(pick_ref[...], whole_ref[...], (0, 0)).astype(jnp.bfloat16)

    width = pieces[0].shape[1]
    shape = (len(pieces) * pieces[0].shape[0], width)
    outs = [(shape, jnp.bfloat16), ((pick.shape[1], width), jnp.bfloat16)]
    return call_kernel(body, outs, [], *pieces, pick)


def expert_lanes(slots):
    expert = lax.broadcasted_iota(jnp.int32, (slots, LANES), 0) // CAP
    return lax.broadcasted_iota(jnp.int32, (slots, LANES), 1) == expert


def token_rows(pieces, pick, router, chosen):
    narrow = jnp.bfloat16
    width = pieces[0].shape[1]
    slots = pick.shape[1]

    def body(*refs):
        pick_ref, router_ref, chosen_ref, whole_ref, rows_ref = refs[-5:]
        assemble(refs[:-5], whole_ref)
        logits = dot_of(whole_ref[...], router_ref[...], (1, 0))
        shifted = jnp.exp(logits - jnp.max(logits, axis=1, keepdims=True))
        route = shifted / jnp.sum(shifted, axis=1, keepdims=True)
        gate = jnp.where(chosen_ref[...] > 0, route[:, :ACTIVE], 0.0)
        high = gate.astype(narrow)
        low = (gate - high.astype(jnp.float32)).astype(narrow)
        rows_ref[:, :width] = dot_of(pick_ref[...], whole_ref[...], (0, 0)).astype(narrow)
        expert = lax.broadcasted_iota(jnp.int32, (slots, ACTIVE), 0) // CAP
        own = lax.broadcasted_iota(jnp.int32, (slots, ACTIVE), 1) == expert
        high, low = [
            jnp.sum(jnp.where(own, dot_of(pick_ref[...], part, (0, 0)), 0.0), axis=1, keepdims=True)
            for part in (high, low)
        ]
        rows_ref[:, width:] = two_lanes(high, low)

    shape = (len(pieces) * pieces[0].shape[0], width)
    outs = [(shape, narrow), ((slots, width + LANES), narrow)]
    return call_kernel(body, outs, [], *pieces, pick, router, chosen)


def two_lanes(high, low):
    lane = lax.broadcasted_iota(jnp.int32, (high.shape[0], LANES), 1)
    return jnp.where(lane == 0, high, jnp.where(lane == 1, low, 0.0)).astype(jnp.bfloat16)


def combined_rows(pick, back, share):
    narrow = jnp.bfloat16
    rows, width = share.shape
    slots = pick.shape[1]

    def body(pick_ref, back_ref, share_ref, out_ref):
        extra = back_ref[:, width:]
        own = expert_lanes(slots)
        spread = [jnp.where(own, extra[:, i : i + 1], 0.0).astype(narrow) for i in range(2)]
        values = share_ref[...] + dot_of(pick_ref[...], back_ref[:, :width], (1, 0))
        out_ref[:, :width] = values.astype(narrow)
        values = dot_of(pick_ref[...], spread[0], (1, 0)) + dot_of(pick_ref[...], spread[1], (1, 0))
        out_ref[:, width:] = values.astype(narrow)

    return call_kernel(body, [((rows, width + LANES), narrow)], [], pick, back, share)[0]


def block(
    block_in,
    attn_norm_gain,
    query_weight,
    kv_down_weight,
    latent_gain,
    kv_up_weight,
    output_weight,
    ffn_norm_gain,
    router_weight,
    expert_ids,
    shared_gate_weight,
    shared_up_weight,
    shared_down_weight,
    expert_gate_weight,
    expert_up_weight,
    expert_down_weight,
    out_grad,
):
    wide = jnp.float32
    narrow = jnp.bfloat16
    own_rows = block_in.shape[0]
    width = block_in.shape[1]
    dp_count = lax.axis_size(DP)
    tensor_count = lax.axis_size(TENSOR)
    tensor_index = lax.axis_index(TENSOR)
    group = own_rows * tensor_count
    owner_count = dp_count // ACTIVE
    slot_piece = CAP // owner_count
    slots = ACTIVE * CAP
    both = (DP, TENSOR)
    first_order, second_order = dp_orders()

    in_pieces = gather_tensor(block_in)
    small = jnp.concatenate([kv_down_weight, router_weight], axis=1)
    small = exchange(jnp.broadcast_to(small[None], (tensor_count,) + small.shape), TENSOR)
    gains = jnp.concatenate([attn_norm_gain, ffn_norm_gain, latent_gain])
    gains = exchange(
        jnp.broadcast_to(gains[None], (dp_count * tensor_count, gains.shape[0])), both
    ).astype(wide)
    split_one = attn_norm_gain.shape[0]
    gain_one = gains[:, :split_one].reshape(-1)
    gain_two = gains[:, split_one : 2 * split_one].reshape(-1)
    gain_lat = gains[:, 2 * split_one :].reshape(-1)

    query_full = gather_dp(query_weight, first_order)
    query_full = query_full.reshape(width, -1)
    small = gather_dp(small, second_order).reshape(width, -1)
    kv_up_full = gather_dp(kv_up_weight, second_order).reshape(LATENT, -1)
    kv_down = small[:, : LATENT + ROPE]
    router = small[:, LATENT + ROPE :]
    output_full = gather_dp(output_weight, second_order)
    output_full = wide_rows(output_full)
    grad_pieces = gather_tensor(out_grad, 1)

    shared_units = shared_down_weight.shape[0]
    half = shared_units // 2
    packed = (
        jnp.concatenate([shared_gate_weight.T, shared_down_weight[:half]]),
        jnp.concatenate([shared_up_weight.T, shared_down_weight[half:]]),
    )
    shared = (
        gather_dp(packed[0], first_order, apart=True),
        gather_dp(packed[1], second_order, apart=True),
    )
    units = expert_down_weight.shape[1]
    slabs = jnp.concatenate(
            [
                jnp.swapaxes(expert_gate_weight, 1, 2),
                jnp.swapaxes(expert_up_weight, 1, 2),
                expert_down_weight,
            ],
            axis=1,
    )
    slabs = exchange(jnp.repeat(slabs, owner_count, axis=0), DP)

    heads = query_full.shape[1] // (NOPE + ROPE)
    all_in, hidden_one = normed_rows(in_pieces, gain_one)
    latent_in = matmul(hidden_one, kv_down).astype(narrow)
    compressed = latent_in[:, :LATENT].astype(wide)
    scale_lat = rms_scale(compressed)
    normed_lat = compressed * scale_lat
    latent = (normed_lat * gain_lat).astype(narrow)
    place = (jnp.arange(group) + tensor_index * own_rows) % group
    position = (place % SEQ).astype(wide)
    sequence = place // SEQ
    seen = (place[:, None] >= place[None, :]) & (sequence[:, None] == sequence[None, :])
    cosine, sine = rope_tables(position)
    key_rope = rotate(latent_in[:, LATENT:].astype(wide), cosine, sine).astype(narrow)
    query = matmul(hidden_one, query_full).reshape(group, heads, NOPE + ROPE)
    query_nope = query[..., :NOPE].astype(narrow)
    query_rope = rotate(query[..., NOPE:], cosine[:, None, :], sine[:, None, :]).astype(narrow)
    keyvalue = matmul(latent, kv_up_full).astype(narrow).reshape(group, heads, NOPE + VDIM)
    key_nope = keyvalue[..., :NOPE]
    values = keyvalue[..., NOPE:]
    mixed, logsum = attend_forward(query_nope, query_rope, key_nope, key_rope, values, seen)
    mixed_flat = mixed.reshape(group, heads * VDIM)
    attn_share = matmul(mixed_flat, output_full)
    attn_own = scatter_tensor(attn_share)

    residual_in = block_in.astype(wide)
    after_attn = residual_in + attn_own
    scale_two = rms_scale(after_attn)
    normed_two = after_attn * scale_two
    hidden_two_own = (normed_two * gain_two).astype(narrow)
    hidden_pieces = gather_tensor(hidden_two_own)

    ids = jnp.concatenate([expert_ids, expert_ids], axis=0)
    ids = lax.dynamic_slice_in_dim(ids, tensor_index * own_rows, group, 0)
    chosen = jnp.any(ids[:, :, None] == jnp.arange(ACTIVE, dtype=jnp.int32)[None, None, :], axis=1)
    ranks = jnp.cumsum(chosen.astype(jnp.int32), axis=0) - 1
    places = (ranks[:, :, None] == jnp.arange(CAP, dtype=jnp.int32)[None, None, :]) & chosen[
        :, :, None
    ]
    pick = places.astype(narrow).reshape(group, slots)
    grad_all, grad_in = picked_rows(grad_pieces, pick)
    grad_here = exchange(grad_in.reshape(dp_count, slot_piece, width), DP).reshape(-1, width)
    hidden_two, tokens_in = token_rows(hidden_pieces, pick, router, chosen.astype(jnp.int32))
    rows_here = exchange(tokens_in.reshape(dp_count, slot_piece, -1), DP)
    rows_here = rows_here.reshape(slots, -1)

    moe_share, hidden_two_share, shared_first, shared_second = shared_experts(
            hidden_two, grad_all, shared[0], shared[1], shared_units, lax.axis_index(DP) & 1
    )

    owned_back, owned_a_grad, owned_b_grad, owned_scaled = owned_first(rows_here, grad_here, slabs)
    back_flat = exchange(owned_back.reshape(dp_count, slot_piece, -1), DP)
    back_flat = back_flat.reshape(slots, -1)
    owned_out, terms = owned_second(
            rows_here, grad_here, slabs, owned_a_grad, owned_b_grad, owned_scaled
    )
    routed_flat = exchange(owned_out.reshape(dp_count, slot_piece, width), DP).reshape(-1, width)
    terms = exchange(terms, DP)
    terms = terms.reshape((ACTIVE, owner_count) + terms.shape[1:])

    def summed(first):
        return jnp.sum(terms[:, :, first : first + units].astype(wide), axis=1)

    expert_gate_grad = jnp.swapaxes(summed(0), 1, 2)
    expert_up_wgrad = jnp.swapaxes(summed(units), 1, 2)
    expert_down_grad = summed(2 * units)

    hidden_two_share = combined_rows(pick, back_flat, hidden_two_share)
    hidden_two_grad = scatter_tensor(hidden_two_share)
    gate_grad = hidden_two_grad[:, width : width + ACTIVE]
    hidden_two_grad = hidden_two_grad[:, :width]
    prob_own = jax.nn.softmax(matmul(hidden_two_own, router), axis=-1)
    prob_grad = jnp.concatenate(
        [gate_grad, jnp.zeros((own_rows, prob_own.shape[1] - ACTIVE), wide)], axis=-1
    )
    logit_grad = (
        prob_own * (prob_grad - jnp.sum(prob_own * prob_grad, axis=-1, keepdims=True))
    ).astype(narrow)
    hidden_two_grad = hidden_two_grad + right_dot(logit_grad, router)
    gain_two_grad = jnp.sum(hidden_two_grad * normed_two, axis=0)
    after_attn_grad = out_grad.astype(wide) + norm_back(
            hidden_two_grad * gain_two, normed_two, scale_two
    )
    residual_low = gather_tensor(after_attn_grad.astype(narrow))
    residual_low = joined(residual_low)
    moe_share = moe_share.astype(wide) + matmul(pick, routed_flat)
    moe_own = scatter_tensor(moe_share, 1)
    block_out = (after_attn + moe_own).astype(narrow)

    mixed_grad = right_dot(residual_low, output_full).astype(narrow).reshape(group, heads, VDIM)
    output_grad = left_dot(mixed_flat, residual_low)
    query_nope_grad, query_rope_grad, key_nope_grad, key_rope_grad, values_grad = attend_backward(
            query_nope, query_rope, key_nope, key_rope, values, mixed, mixed_grad, logsum, seen
    )
    keyvalue_grad = (
        jnp.concatenate([key_nope_grad, values_grad], axis=-1)
        .astype(narrow)
        .reshape(group, heads * (NOPE + VDIM))
    )
    latent_grad = right_dot(keyvalue_grad, kv_up_full)
    gain_lat_grad = jnp.sum(latent_grad * normed_lat, axis=0)
    compressed_grad = norm_back(latent_grad * gain_lat, normed_lat, scale_lat)
    key_rope_back = unrotate(key_rope_grad, cosine, sine)
    latent_in_share = jnp.concatenate([compressed_grad, key_rope_back], axis=-1)
    latent_in_low = latent_in_share.astype(narrow)
    query_rope_back = unrotate(query_rope_grad, cosine[:, None, :], sine[:, None, :])
    query_grad = (
        jnp.concatenate([query_nope_grad, query_rope_back], axis=-1)
        .astype(narrow)
        .reshape(group, heads * (NOPE + ROPE))
    )
    hidden_one_share = right_dot(query_grad, query_full) + right_dot(latent_in_low, kv_down)
    hidden_one_grad = scatter_tensor(hidden_one_share)
    query_wgrad = left_dot(hidden_one, query_grad)
    kv_up_grad = left_dot(latent, keyvalue_grad)
    scale_one = rms_scale(residual_in)
    normed_one = residual_in * scale_one
    input_grad = after_attn_grad + norm_back(hidden_one_grad * gain_one, normed_one, scale_one)

    latent_wide = jnp.pad(latent_in_low, ((0, 0), (0, router.shape[1])))
    logit_wide = jnp.pad(logit_grad, ((0, 0), (latent_in_low.shape[1], 0)))
    tall = left_dot(hidden_one, latent_wide) + left_dot(hidden_two_own, logit_wide)
    tall = tall.astype(narrow)
    tall = tall.reshape(dp_count, -1, tall.shape[1])
    shared_first = scatter_dp(shared_first, first_order)
    shared_second = scatter_dp(shared_second, second_order)
    shared_grads = (
        shared_first[:shared_units].T,
        shared_second[:shared_units].T,
        jnp.concatenate([shared_first[shared_units:], shared_second[shared_units:]]),
    )
    output_grad = scatter_dp(tall_blocks(output_grad), second_order)
    query_wgrad = query_wgrad.astype(narrow).reshape(dp_count, -1, query_wgrad.shape[1])
    query_wgrad = scatter_dp(query_wgrad, first_order)
    kv_up_grad = kv_up_grad.astype(narrow).reshape(dp_count, -1, kv_up_grad.shape[1])
    kv_up_grad = scatter_dp(kv_up_grad, second_order)
    tall = scatter_dp(tall, second_order).astype(narrow)
    tall = exchange(tall.reshape(tensor_count, -1, tall.shape[1]), TENSOR)
    tall = jnp.sum(tall.astype(wide), axis=0)
    kv_down_grad = tall[:, : LATENT + ROPE]
    router_grad = tall[:, LATENT + ROPE :]
    residual_all = all_in.astype(wide)
    gain_one_grad = jnp.sum(
        hidden_one_share * (residual_all * rms_scale(residual_all)), axis=0
    )
    devices = dp_count * tensor_count
    gain_grads = jnp.concatenate(
        [
            gain_one_grad.reshape(devices, -1),
            gain_two_grad.reshape(devices, -1),
            gain_lat_grad.reshape(devices, -1),
        ],
        axis=1,
    )
    gain_grads = jnp.sum(exchange(gain_grads, both), axis=0)
    return (
        block_out,
        input_grad,
        gain_grads[:split_one],
        query_wgrad,
        kv_down_grad,
        gain_grads[2 * split_one :],
        kv_up_grad,
        output_grad,
        gain_grads[split_one : 2 * split_one],
        router_grad,
        shared_grads[0],
        shared_grads[1],
        shared_grads[2],
        expert_gate_grad,
        expert_up_wgrad,
        expert_down_grad,
    )


def solution(mesh):
    in_specs = (
        P((DP, TENSOR), None),
        P((DP, TENSOR)),
        P(DP, TENSOR),
        P((DP, TENSOR), None),
        P((DP, TENSOR)),
        P(DP, TENSOR),
        P(TENSOR, DP),
        P((DP, TENSOR)),
        P((DP, TENSOR), None),
        P(DP, None),
        P(DP, TENSOR),
        P(DP, TENSOR),
        P(TENSOR, DP),
        P(None, DP, TENSOR),
        P(None, DP, TENSOR),
        P(None, TENSOR, DP),
        P((DP, TENSOR), None),
    )
    out_specs = (
        P((DP, TENSOR), None),
        P((DP, TENSOR), None),
        P((DP, TENSOR)),
        P(DP, TENSOR),
        P((DP, TENSOR), None),
        P((DP, TENSOR)),
        P(DP, TENSOR),
        P(TENSOR, DP),
        P((DP, TENSOR)),
        P((DP, TENSOR), None),
        P(DP, TENSOR),
        P(DP, TENSOR),
        P(TENSOR, DP),
        P(None, DP, TENSOR),
        P(None, DP, TENSOR),
        P(None, TENSOR, DP),
    )
    return jax.shard_map(block, mesh=mesh, in_specs=in_specs, out_specs=out_specs, check_vma=False)
```

```python
import jax
import jax.numpy as jnp
from jax import lax
from jax.experimental import pallas as pl
from jax.experimental.pallas import tpu as pltpu
from jax.sharding import PartitionSpec as P

NOPE = 128
ROPE = 64
VDIM = 128
LATENT = 512
ACTIVE = 8
SEQ = 512
CAP = 96


LANES = 128
DP = "dp"
TENSOR = "tensor"
EPSILON = 1e-06
NEGATIVE = -1e30


def matmul(left, right):
    return jnp.dot(left, right, preferred_element_type=jnp.float32)


def left_dot(left, right):
    return lax.dot_general(
        left, right, (((0,), (0,)), ((), ())), preferred_element_type=jnp.float32
    )


def right_dot(left, right):
    return lax.dot_general(
        left, right, (((left.ndim - 1,), (1,)), ((), ())), preferred_element_type=jnp.float32
    )


def einsum32(form, left, right):
    return jnp.einsum(form, left, right, preferred_element_type=jnp.float32)


def rms_scale(values):
    return lax.rsqrt(jnp.mean(values * values, axis=-1, keepdims=True) + EPSILON)


def norm_back(grad_normed, normed, scale):
    return scale * (grad_normed - normed * jnp.mean(grad_normed * normed, axis=-1, keepdims=True))


def rope_tables(position):
    halfway = ROPE // 2
    inverse = jnp.exp(-jnp.log(10000.0) * jnp.arange(halfway).astype(jnp.float32) / halfway)
    angles = position[:, None] * inverse[None, :]
    return (jnp.cos(angles), jnp.sin(angles))


def rotate(values, cosine, sine):
    halfway = ROPE // 2
    first, second = (values[..., :halfway], values[..., halfway:])
    return jnp.concatenate(
        [first * cosine - second * sine, first * sine + second * cosine], axis=-1
    )


def unrotate(grads, cosine, sine):
    halfway = ROPE // 2
    first, second = (grads[..., :halfway], grads[..., halfway:])
    return jnp.concatenate(
        [first * cosine + second * sine, second * cosine - first * sine], axis=-1
    )


def send_tensor(values, step):
    count = lax.axis_size(TENSOR)
    return lax.ppermute(values, TENSOR, [(i, (i + step) % count) for i in range(count)])


def pieces_of(values, parts):
    rows = values.shape[0] // parts
    return [values[i * rows : (i + 1) * rows] for i in range(parts)]


def gather_tensor(own, parts=2):
    pieces = pieces_of(own, parts)
    found = list(pieces)
    for _ in range(1, lax.axis_size(TENSOR)):
        pieces = [send_tensor(piece, -1) for piece in pieces]
        found += pieces
    return found


def scatter_tensor(share, parts=2):
    count = lax.axis_size(TENSOR)
    blocks = share.reshape((count, share.shape[0] // count) + share.shape[1:])
    sums = [piece.astype(jnp.bfloat16) for piece in pieces_of(blocks[count - 1], parts)]
    for step in range(1, count):
        sums = [send_tensor(piece, 1) for piece in sums]
        sums = [
            piece.astype(jnp.float32) + more.astype(jnp.float32)
            for piece, more in zip(sums, pieces_of(blocks[count - 1 - step], parts))
        ]
        if step < count - 1:
            sums = [piece.astype(jnp.bfloat16) for piece in sums]
    return jnp.concatenate(sums, axis=0)


def exchange(values, axes):
    return lax.all_to_all(values, axes, split_axis=0, concat_axis=0, tiled=True)


def dp_orders():
    count = lax.axis_size(DP)
    masks = [1 << k for k in range(count.bit_length() - 1)]
    return (masks[1:] + masks[:1], masks[:0:-1] + masks[:1])


def swap_dp(values, mask):
    count = lax.axis_size(DP)
    return lax.ppermute(values, DP, [(i, i ^ mask) for i in range(count)])


def axis_of(mask):
    return lax.axis_size(DP).bit_length() - 1 - mask.bit_length()


def gather_dp(own, order, apart=False):
    count = lax.axis_size(DP)
    index = lax.axis_index(DP)
    current = own.reshape((1,) * (count.bit_length() - 1) + own.shape)
    for step, mask in enumerate(order):
        other = swap_dp(current, mask)
        if apart and step + 1 == len(order):
            return [values.reshape((count // 2,) + own.shape) for values in (current, other)]
        high = (index & mask) > 0
        current = jnp.concatenate(
            [jnp.where(high, other, current), jnp.where(high, current, other)],
            axis=axis_of(mask),
        )
    return current.reshape((count,) + own.shape)


def scatter_dp(blocks, order):
    count = lax.axis_size(DP)
    index = lax.axis_index(DP)
    bits = count.bit_length() - 1
    pair = isinstance(blocks, (tuple, list))
    own = blocks[0].shape[1:] if pair else blocks.shape[1:]
    current = None if pair else blocks.reshape((2,) * bits + own)
    for step, mask in enumerate(order[::-1]):
        high = ((index & mask) > 0).astype(jnp.int32)
        axis = axis_of(mask)
        if current is None:
            keep, give = [half.reshape((2,) * (bits - 1) + (1,) + own) for half in blocks]
        else:
            keep = lax.dynamic_slice_in_dim(current, high, 1, axis)
            give = lax.dynamic_slice_in_dim(current, 1 - high, 1, axis).astype(jnp.bfloat16)
        got = swap_dp(give, mask)
        current = keep.astype(jnp.float32) + got.astype(jnp.float32)
        if step + 1 < bits:
            current = current.astype(jnp.bfloat16)
    return current.reshape(own)


def wide_rows(blocks):
    return jnp.moveaxis(blocks, 0, 1).reshape(blocks.shape[1], -1)


def tall_blocks(values):
    count = lax.axis_size(DP)
    values = values.reshape(values.shape[0], count, -1)
    return jnp.moveaxis(values, 1, 0).astype(jnp.bfloat16)


def causal_scores(query_nope, query_rope, key_nope, key_rope, seen):
    scores = einsum32("qhd,khd->hqk", query_nope, key_nope)
    scores = scores + einsum32("qhd,kd->hqk", query_rope, key_rope)
    return jnp.where(seen[None], scores * (NOPE + ROPE) ** (-0.5), NEGATIVE)


def attend_forward(query_nope, query_rope, key_nope, key_rope, values, seen):
    scores = causal_scores(query_nope, query_rope, key_nope, key_rope, seen)
    logsum = jax.nn.logsumexp(scores, axis=-1)
    probs = jnp.exp(scores - logsum[..., None]).astype(jnp.bfloat16)
    return (einsum32("hqk,khd->qhd", probs, values).astype(jnp.bfloat16), logsum)


def attend_backward(
    query_nope, query_rope, key_nope, key_rope, values, mixed, mixed_grad, logsum, seen
):
    scores = causal_scores(query_nope, query_rope, key_nope, key_rope, seen)
    probs_full = jnp.exp(scores - logsum[..., None])
    probs = probs_full.astype(jnp.bfloat16)
    values_grad = einsum32("hqk,qhd->khd", probs, mixed_grad)
    probs_grad = einsum32("qhd,khd->hqk", mixed_grad, values)
    delta = einsum32("qhd,qhd->hq", mixed_grad, mixed)
    score_grad = (probs_full * (probs_grad - delta[..., None]) * (NOPE + ROPE) ** (-0.5)).astype(
        jnp.bfloat16
    )
    query_nope_grad = einsum32("hqk,khd->qhd", score_grad, key_nope)
    query_rope_grad = einsum32("hqk,kd->qhd", score_grad, key_rope)
    key_nope_grad = einsum32("hqk,qhd->khd", score_grad, query_nope)
    key_rope_grad = einsum32("hqk,qhd->kd", score_grad, query_rope)
    return (query_nope_grad, query_rope_grad, key_nope_grad, key_rope_grad, values_grad)


def regroup(blocks, count):
    if blocks.shape[0] == count:
        return blocks
    values = jnp.moveaxis(blocks, 0, 1).reshape(blocks.shape[1], count, -1)
    return jnp.moveaxis(values, 1, 0)


def lane_count(blocks):
    return min(blocks.shape[0], blocks.shape[0] * blocks.shape[2] // LANES)


def dot_of(left, right, dims):
    return lax.dot_general(left, right, ((dims[:1], dims[1:]), ((), ())), preferred_element_type=jnp.float32)


def swiglu_parts(first, second, grad):
    sigma = 1.0 / (1.0 + jnp.exp(-first))
    gated = first * sigma
    return (gated * second, grad * second * (sigma * (1.0 + first * (1.0 - sigma))), grad * gated)


def call_kernel(body, outs, scratch, *arguments):
    return pl.pallas_call(
        body,
        out_shape=[jax.ShapeDtypeStruct(shape, dtype) for shape, dtype in outs],
        scratch_shapes=[pltpu.VMEM(shape, dtype) for shape, dtype in scratch],
    )(*arguments)


def mingle(pair, bit):
    mine, theirs = pair
    blocks = [jnp.where(bit > 0, theirs, mine), jnp.where(bit > 0, mine, theirs)]
    return jnp.stack(blocks, axis=1).reshape((-1,) + mine.shape[1:])


def part_by(blocks, bit):
    even, odd = blocks[0::2], blocks[1::2]
    return [jnp.where(bit > 0, odd, even), jnp.where(bit > 0, even, odd)]


def shared_experts(hidden, grad, firsts, seconds, units, bit):
    if firsts[0].shape[2] % LANES == 0:
        return shared_kernel(hidden, grad, firsts, seconds, units, bit)
    first, second = [mingle(pair, bit) for pair in (firsts, seconds)]
    given, count = first.shape[0], lane_count(first)
    pairs = [part_by(regroup(blocks, count), 0) for blocks in (first, second)]
    out, back, *pairs = shared_kernel(hidden, grad, *pairs, units, jnp.int32(0))
    pairs = [part_by(regroup(mingle(pair, 0), given), bit) for pair in pairs]
    return out, back, *pairs


def shared_kernel(hidden, grad, firsts, seconds, units, bit):
    narrow = jnp.bfloat16
    rows, width = hidden.shape
    count, _, part = firsts[0].shape
    half = units // 2

    def body(bit_ref, x_ref, g_ref, *refs):
        pairs, (out_ref, back_ref), results = refs[:4], refs[4:6], refs[6:10]
        gate_ref, up_ref, down_ref = refs[10:]
        mine = bit_ref[0]
        for j in range(count):
            for place in range(2):
                own = mine if place == 0 else 1 - mine
                lanes = pl.ds(pl.multiple_of((2 * j + own) * part, LANES), part)
                gate_ref[:, lanes] = pairs[place][j, :units]
                up_ref[:, lanes] = pairs[2 + place][j, :units]
                down_ref[:half, lanes] = pairs[place][j, units:]
                down_ref[half:, lanes] = pairs[2 + place][j, units:]
        a = dot_of(x_ref[...], gate_ref[...], (1, 1))
        b = dot_of(x_ref[...], up_ref[...], (1, 1))
        u = dot_of(g_ref[...], down_ref[...], (1, 1))
        h, da, db = [v.astype(narrow) for v in swiglu_parts(a, b, u)]
        out_ref[...] = dot_of(h, down_ref[...], (1, 0)).astype(narrow)
        back_ref[...] = dot_of(da, gate_ref[...], (1, 0)) + dot_of(db, up_ref[...], (1, 0))
        gate_ref[...] = dot_of(da, x_ref[...], (0, 0)).astype(narrow)
        up_ref[...] = dot_of(db, x_ref[...], (0, 0)).astype(narrow)
        down_ref[...] = dot_of(h, g_ref[...], (0, 0)).astype(narrow)
        for j in range(count):
            for place in range(2):
                own = mine if place == 0 else 1 - mine
                lanes = pl.ds(pl.multiple_of((2 * j + own) * part, LANES), part)
                results[place][j, :units] = gate_ref[:, lanes]
                results[2 + place][j, :units] = up_ref[:, lanes]
                results[place][j, units:] = down_ref[:half, lanes]
                results[2 + place][j, units:] = down_ref[half:, lanes]

    blocks = (firsts[0].shape, narrow)
    vmem = pl.BlockSpec(memory_space=pltpu.VMEM)
    out, back, *results = pl.pallas_call(
        body,
        in_specs=[pl.BlockSpec(memory_space=pltpu.SMEM)] + [vmem] * 6,
        out_shape=[
            jax.ShapeDtypeStruct(shape, dtype)
            for shape, dtype in [((rows, width), narrow), ((rows, width), jnp.float32)] + [blocks] * 4
        ],
        scratch_shapes=[pltpu.VMEM((units, width), narrow)] * 3,
    )(bit.reshape(1), hidden, grad, *firsts, *seconds)
    return out, back, results[:2], results[2:]


def column_gradient(left, right, bit):
    count = lax.axis_size(DP)
    rows, width = left.shape[1], right.shape[1]
    part = width // count
    if part % LANES:
        return part_by(tall_blocks(left_dot(left, right)), bit)

    def body(bit_ref, left_ref, right_ref, keep_ref, give_ref, whole_ref):
        whole_ref[...] = dot_of(left_ref[...], right_ref[...], (0, 0)).astype(jnp.bfloat16)
        for j in range(count // 2):
            for ref, own in ((keep_ref, bit_ref[0]), (give_ref, 1 - bit_ref[0])):
                ref[j] = whole_ref[:, pl.ds(pl.multiple_of((2 * j + own) * part, LANES), part)]

    vmem = pl.BlockSpec(memory_space=pltpu.VMEM)
    return pl.pallas_call(
        body,
        in_specs=[pl.BlockSpec(memory_space=pltpu.SMEM), vmem, vmem],
        out_shape=[jax.ShapeDtypeStruct((count // 2, rows, part), jnp.bfloat16)] * 2,
        scratch_shapes=[pltpu.VMEM((rows, width), jnp.bfloat16)],
    )(bit.reshape(1), left, right)


def load_slab(slab_ref, wide_ref, place, units):
    part = slab_ref.shape[2]
    for j in range(slab_ref.shape[0]):
        wide_ref[:, j * part : (j + 1) * part] = slab_ref[j, place * units : (place + 1) * units]


def owned_first(rows, grads, slabs):
    narrow = jnp.bfloat16
    slots, width = grads.shape
    units = slabs.shape[1] // 3
    slabs = regroup(slabs, lane_count(slabs))

    def body(x_ref, g_ref, slab_ref, back_ref, da_ref, db_ref, scaled_ref, gate_ref, up_ref, down_ref):
        load_slab(slab_ref, gate_ref, 0, units)
        load_slab(slab_ref, up_ref, 1, units)
        load_slab(slab_ref, down_ref, 2, units)
        x = x_ref[:, :width]
        extra = x_ref[:, width:].astype(jnp.float32)
        weight = extra[:, 0:1] + extra[:, 1:2]
        a = dot_of(x, gate_ref[...], (1, 1))
        b = dot_of(x, up_ref[...], (1, 1))
        u = dot_of(g_ref[...], down_ref[...], (1, 1))
        h, da, db = swiglu_parts(a, b, u)
        h = h.astype(narrow).astype(jnp.float32)
        slot = jnp.sum(u * h, axis=1, keepdims=True)
        da = (weight * da).astype(narrow)
        db = (weight * db).astype(narrow)
        da_ref[...] = da
        db_ref[...] = db
        scaled_ref[...] = (weight * h).astype(narrow)
        back_ref[:, :width] = (
            dot_of(da, gate_ref[...], (1, 0)) + dot_of(db, up_ref[...], (1, 0))
        ).astype(narrow)
        high = slot.astype(narrow).astype(jnp.float32)
        back_ref[:, width:] = two_lanes(high, slot - high)

    inner = ((slots, units), narrow)
    return call_kernel(
        body, [(rows.shape, narrow), inner, inner, inner], [((units, width), narrow)] * 3,
        rows, grads, slabs,
    )


def owned_second(rows, grads, slabs, da, db, scaled):
    narrow = jnp.bfloat16
    slots, width = grads.shape
    units = slabs.shape[1] // 3
    given = slabs.shape[0]
    slabs = regroup(slabs, lane_count(slabs))

    def body(x_ref, g_ref, slab_ref, da_ref, db_ref, scaled_ref, out_ref, term_ref, down_ref):
        part = slab_ref.shape[2]
        load_slab(slab_ref, down_ref, 2, units)
        out_ref[...] = dot_of(scaled_ref[...], down_ref[...], (1, 0)).astype(narrow)
        x = x_ref[:, :width]
        for place, value in enumerate(
            (dot_of(da_ref[...], x, (0, 0)), dot_of(db_ref[...], x, (0, 0)),
             dot_of(scaled_ref[...], g_ref[...], (0, 0)))
        ):
            for j in range(slab_ref.shape[0]):
                term_ref[j, place * units : (place + 1) * units] = value[
                    :, j * part : (j + 1) * part
                ].astype(narrow)

    out, terms = call_kernel(
        body, [((slots, width), narrow), (slabs.shape, narrow)], [((units, width), narrow)],
        rows, grads, slabs, da, db, scaled,
    )
    return out, regroup(terms, given)


def assemble(refs, whole_ref):
    rows = refs[0].shape[0]
    for i, ref in enumerate(refs):
        whole_ref[i * rows : (i + 1) * rows] = ref[...]


def joined(pieces):
    def body(*refs):
        assemble(refs[:-1], refs[-1])

    shape = (len(pieces) * pieces[0].shape[0], pieces[0].shape[1])
    return call_kernel(body, [(shape, pieces[0].dtype)], [], *pieces)[0]


def normed_rows(pieces, gain):
    def body(*refs):
        gain_ref, whole_ref, hidden_ref = refs[-3:]
        rows = refs[0].shape[0]
        for i, ref in enumerate(refs[:-3]):
            values = ref[...]
            whole_ref[i * rows : (i + 1) * rows] = values
            values = values.astype(jnp.float32)
            hidden_ref[i * rows : (i + 1) * rows] = (
                values * rms_scale(values) * gain_ref[...]
            ).astype(jnp.bfloat16)

    shape = (len(pieces) * pieces[0].shape[0], pieces[0].shape[1])
    return call_kernel(body, [(shape, jnp.bfloat16)] * 2, [], *pieces, gain[None])


def picked_rows(pieces, pick):
    def body(*refs):
        pick_ref, whole_ref, rows_ref = refs[-3:]
        assemble(refs[:-3], whole_ref)
        rows_ref[...] = dot_of(pick_ref[...], whole_ref[...], (0, 0)).astype(jnp.bfloat16)

    width = pieces[0].shape[1]
    shape = (len(pieces) * pieces[0].shape[0], width)
    outs = [(shape, jnp.bfloat16), ((pick.shape[1], width), jnp.bfloat16)]
    return call_kernel(body, outs, [], *pieces, pick)


def expert_lanes(slots):
    expert = lax.broadcasted_iota(jnp.int32, (slots, LANES), 0) // CAP
    return lax.broadcasted_iota(jnp.int32, (slots, LANES), 1) == expert


def token_rows(pieces, pick, router, chosen):
    narrow = jnp.bfloat16
    width = pieces[0].shape[1]
    slots = pick.shape[1]

    def body(*refs):
        pick_ref, router_ref, chosen_ref, whole_ref, rows_ref = refs[-5:]
        assemble(refs[:-5], whole_ref)
        logits = dot_of(whole_ref[...], router_ref[...], (1, 0))
        shifted = jnp.exp(logits - jnp.max(logits, axis=1, keepdims=True))
        route = shifted / jnp.sum(shifted, axis=1, keepdims=True)
        gate = jnp.where(chosen_ref[...] > 0, route[:, :ACTIVE], 0.0)
        high = gate.astype(narrow)
        low = (gate - high.astype(jnp.float32)).astype(narrow)
        rows_ref[:, :width] = dot_of(pick_ref[...], whole_ref[...], (0, 0)).astype(narrow)
        expert = lax.broadcasted_iota(jnp.int32, (slots, ACTIVE), 0) // CAP
        own = lax.broadcasted_iota(jnp.int32, (slots, ACTIVE), 1) == expert
        high, low = [
            jnp.sum(jnp.where(own, dot_of(pick_ref[...], part, (0, 0)), 0.0), axis=1, keepdims=True)
            for part in (high, low)
        ]
        rows_ref[:, width:] = two_lanes(high, low)

    shape = (len(pieces) * pieces[0].shape[0], width)
    outs = [(shape, narrow), ((slots, width + LANES), narrow)]
    return call_kernel(body, outs, [], *pieces, pick, router, chosen)


def two_lanes(high, low):
    lane = lax.broadcasted_iota(jnp.int32, (high.shape[0], LANES), 1)
    return jnp.where(lane == 0, high, jnp.where(lane == 1, low, 0.0)).astype(jnp.bfloat16)


def added_rows(pick, routed, share):
    def body(pick_ref, routed_ref, share_ref, out_ref):
        values = share_ref[...].astype(jnp.float32)
        values = values + dot_of(pick_ref[...], routed_ref[...], (1, 0))
        out_ref[...] = values.astype(jnp.bfloat16)

    return call_kernel(body, [(share.shape, jnp.bfloat16)], [], pick, routed, share)[0]


def combined_rows(pick, back, share):
    narrow = jnp.bfloat16
    rows, width = share.shape
    slots = pick.shape[1]

    def body(pick_ref, back_ref, share_ref, out_ref):
        extra = back_ref[:, width:]
        own = expert_lanes(slots)
        spread = [jnp.where(own, extra[:, i : i + 1], 0.0).astype(narrow) for i in range(2)]
        values = share_ref[...] + dot_of(pick_ref[...], back_ref[:, :width], (1, 0))
        out_ref[:, :width] = values.astype(narrow)
        values = dot_of(pick_ref[...], spread[0], (1, 0)) + dot_of(pick_ref[...], spread[1], (1, 0))
        out_ref[:, width:] = values.astype(narrow)

    return call_kernel(body, [((rows, width + LANES), narrow)], [], pick, back, share)[0]


def block(
    block_in,
    attn_norm_gain,
    query_weight,
    kv_down_weight,
    latent_gain,
    kv_up_weight,
    output_weight,
    ffn_norm_gain,
    router_weight,
    expert_ids,
    shared_gate_weight,
    shared_up_weight,
    shared_down_weight,
    expert_gate_weight,
    expert_up_weight,
    expert_down_weight,
    out_grad,
):
    wide = jnp.float32
    narrow = jnp.bfloat16
    own_rows = block_in.shape[0]
    width = block_in.shape[1]
    dp_count = lax.axis_size(DP)
    tensor_count = lax.axis_size(TENSOR)
    tensor_index = lax.axis_index(TENSOR)
    group = own_rows * tensor_count
    owner_count = dp_count // ACTIVE
    slot_piece = CAP // owner_count
    slots = ACTIVE * CAP
    both = (DP, TENSOR)
    first_order, second_order = dp_orders()

    in_pieces = gather_tensor(block_in)
    small = jnp.concatenate([kv_down_weight, router_weight], axis=1)
    small = exchange(jnp.broadcast_to(small[None], (tensor_count,) + small.shape), TENSOR)
    gains = jnp.concatenate([attn_norm_gain, ffn_norm_gain, latent_gain])
    gains = exchange(
        jnp.broadcast_to(gains[None], (dp_count * tensor_count, gains.shape[0])), both
    ).astype(wide)
    split_one = attn_norm_gain.shape[0]
    gain_one = gains[:, :split_one].reshape(-1)
    gain_two = gains[:, split_one : 2 * split_one].reshape(-1)
    gain_lat = gains[:, 2 * split_one :].reshape(-1)

    query_full = gather_dp(query_weight, first_order)
    query_full = query_full.reshape(width, -1)
    small = gather_dp(small, second_order).reshape(width, -1)
    kv_up_full = gather_dp(kv_up_weight, second_order).reshape(LATENT, -1)
    kv_down = small[:, : LATENT + ROPE]
    router = small[:, LATENT + ROPE :]
    output_full = gather_dp(output_weight, second_order)
    output_full = wide_rows(output_full)
    grad_pieces = gather_tensor(out_grad, 1)

    shared_units = shared_down_weight.shape[0]
    half = shared_units // 2
    packed = (
        jnp.concatenate([shared_gate_weight.T, shared_down_weight[:half]]),
        jnp.concatenate([shared_up_weight.T, shared_down_weight[half:]]),
    )
    shared = (
        gather_dp(packed[0], first_order, apart=True),
        gather_dp(packed[1], second_order, apart=True),
    )
    units = expert_down_weight.shape[1]
    slabs = jnp.concatenate(
            [
                jnp.swapaxes(expert_gate_weight, 1, 2),
                jnp.swapaxes(expert_up_weight, 1, 2),
                expert_down_weight,
            ],
            axis=1,
    )
    slabs = exchange(jnp.repeat(slabs, owner_count, axis=0), DP)

    heads = query_full.shape[1] // (NOPE + ROPE)
    all_in, hidden_one = normed_rows(in_pieces, gain_one)
    latent_in = matmul(hidden_one, kv_down).astype(narrow)
    compressed = latent_in[:, :LATENT].astype(wide)
    scale_lat = rms_scale(compressed)
    normed_lat = compressed * scale_lat
    latent = (normed_lat * gain_lat).astype(narrow)
    place = (jnp.arange(group) + tensor_index * own_rows) % group
    position = (place % SEQ).astype(wide)
    sequence = place // SEQ
    seen = (place[:, None] >= place[None, :]) & (sequence[:, None] == sequence[None, :])
    cosine, sine = rope_tables(position)
    key_rope = rotate(latent_in[:, LATENT:].astype(wide), cosine, sine).astype(narrow)
    query = matmul(hidden_one, query_full).reshape(group, heads, NOPE + ROPE)
    query_nope = query[..., :NOPE].astype(narrow)
    query_rope = rotate(query[..., NOPE:], cosine[:, None, :], sine[:, None, :]).astype(narrow)
    keyvalue = matmul(latent, kv_up_full).astype(narrow).reshape(group, heads, NOPE + VDIM)
    key_nope = keyvalue[..., :NOPE]
    values = keyvalue[..., NOPE:]
    mixed, logsum = attend_forward(query_nope, query_rope, key_nope, key_rope, values, seen)
    mixed_flat = mixed.reshape(group, heads * VDIM)
    attn_share = matmul(mixed_flat, output_full)
    attn_own = scatter_tensor(attn_share)

    residual_in = block_in.astype(wide)
    after_attn = residual_in + attn_own
    scale_two = rms_scale(after_attn)
    normed_two = after_attn * scale_two
    hidden_two_own = (normed_two * gain_two).astype(narrow)
    hidden_pieces = gather_tensor(hidden_two_own)

    ids = jnp.concatenate([expert_ids, expert_ids], axis=0)
    ids = lax.dynamic_slice_in_dim(ids, tensor_index * own_rows, group, 0)
    chosen = jnp.any(ids[:, :, None] == jnp.arange(ACTIVE, dtype=jnp.int32)[None, None, :], axis=1)
    ranks = jnp.cumsum(chosen.astype(jnp.int32), axis=0) - 1
    places = (ranks[:, :, None] == jnp.arange(CAP, dtype=jnp.int32)[None, None, :]) & chosen[
        :, :, None
    ]
    pick = places.astype(narrow).reshape(group, slots)
    grad_all, grad_in = picked_rows(grad_pieces, pick)
    grad_here = exchange(grad_in.reshape(dp_count, slot_piece, width), DP).reshape(-1, width)
    hidden_two, tokens_in = token_rows(hidden_pieces, pick, router, chosen.astype(jnp.int32))
    rows_here = exchange(tokens_in.reshape(dp_count, slot_piece, -1), DP)
    rows_here = rows_here.reshape(slots, -1)

    moe_share, hidden_two_share, shared_first, shared_second = shared_experts(
            hidden_two, grad_all, shared[0], shared[1], shared_units, lax.axis_index(DP) & 1
    )

    owned_back, owned_a_grad, owned_b_grad, owned_scaled = owned_first(rows_here, grad_here, slabs)
    back_flat = exchange(owned_back.reshape(dp_count, slot_piece, -1), DP)
    back_flat = back_flat.reshape(slots, -1)
    owned_out, terms = owned_second(
            rows_here, grad_here, slabs, owned_a_grad, owned_b_grad, owned_scaled
    )
    routed_flat = exchange(owned_out.reshape(dp_count, slot_piece, width), DP).reshape(-1, width)
    terms = exchange(terms, DP)
    terms = terms.reshape((ACTIVE, owner_count) + terms.shape[1:])

    def summed(first):
        return jnp.sum(terms[:, :, first : first + units].astype(wide), axis=1)

    expert_gate_grad = jnp.swapaxes(summed(0), 1, 2)
    expert_up_wgrad = jnp.swapaxes(summed(units), 1, 2)
    expert_down_grad = summed(2 * units)

    hidden_two_share = combined_rows(pick, back_flat, hidden_two_share)
    hidden_two_grad = scatter_tensor(hidden_two_share)
    gate_grad = hidden_two_grad[:, width : width + ACTIVE]
    hidden_two_grad = hidden_two_grad[:, :width]
    prob_own = jax.nn.softmax(matmul(hidden_two_own, router), axis=-1)
    prob_grad = jnp.concatenate(
        [gate_grad, jnp.zeros((own_rows, prob_own.shape[1] - ACTIVE), wide)], axis=-1
    )
    logit_grad = (
        prob_own * (prob_grad - jnp.sum(prob_own * prob_grad, axis=-1, keepdims=True))
    ).astype(narrow)
    hidden_two_grad = hidden_two_grad + right_dot(logit_grad, router)
    gain_two_grad = jnp.sum(hidden_two_grad * normed_two, axis=0)
    after_attn_grad = out_grad.astype(wide) + norm_back(
            hidden_two_grad * gain_two, normed_two, scale_two
    )
    residual_low = gather_tensor(after_attn_grad.astype(narrow))
    residual_low = joined(residual_low)
    moe_share = added_rows(pick, routed_flat, moe_share)
    moe_own = scatter_tensor(moe_share, 1)
    block_out = (after_attn + moe_own).astype(narrow)

    mixed_grad = right_dot(residual_low, output_full).astype(narrow).reshape(group, heads, VDIM)
    output_grad = column_gradient(mixed_flat, residual_low, lax.axis_index(DP) & 1)
    query_nope_grad, query_rope_grad, key_nope_grad, key_rope_grad, values_grad = attend_backward(
            query_nope, query_rope, key_nope, key_rope, values, mixed, mixed_grad, logsum, seen
    )
    keyvalue_grad = (
        jnp.concatenate([key_nope_grad, values_grad], axis=-1)
        .astype(narrow)
        .reshape(group, heads * (NOPE + VDIM))
    )
    latent_grad = right_dot(keyvalue_grad, kv_up_full)
    gain_lat_grad = jnp.sum(latent_grad * normed_lat, axis=0)
    compressed_grad = norm_back(latent_grad * gain_lat, normed_lat, scale_lat)
    key_rope_back = unrotate(key_rope_grad, cosine, sine)
    latent_in_share = jnp.concatenate([compressed_grad, key_rope_back], axis=-1)
    latent_in_low = latent_in_share.astype(narrow)
    query_rope_back = unrotate(query_rope_grad, cosine[:, None, :], sine[:, None, :])
    query_grad = (
        jnp.concatenate([query_nope_grad, query_rope_back], axis=-1)
        .astype(narrow)
        .reshape(group, heads * (NOPE + ROPE))
    )
    hidden_one_share = right_dot(query_grad, query_full) + right_dot(latent_in_low, kv_down)
    hidden_one_grad = scatter_tensor(hidden_one_share, 1)
    query_wgrad = left_dot(hidden_one, query_grad)
    kv_up_grad = left_dot(latent, keyvalue_grad)
    scale_one = rms_scale(residual_in)
    normed_one = residual_in * scale_one
    input_grad = after_attn_grad + norm_back(hidden_one_grad * gain_one, normed_one, scale_one)

    latent_wide = jnp.pad(latent_in_low, ((0, 0), (0, router.shape[1])))
    logit_wide = jnp.pad(logit_grad, ((0, 0), (latent_in_low.shape[1], 0)))
    tall = left_dot(hidden_one, latent_wide) + left_dot(hidden_two_own, logit_wide)
    tall = tall.astype(narrow)
    tall = tall.reshape(dp_count, -1, tall.shape[1])
    shared_first = scatter_dp(shared_first, first_order)
    shared_second = scatter_dp(shared_second, second_order)
    shared_grads = (
        shared_first[:shared_units].T,
        shared_second[:shared_units].T,
        jnp.concatenate([shared_first[shared_units:], shared_second[shared_units:]]),
    )
    output_grad = scatter_dp(output_grad, second_order)
    query_wgrad = query_wgrad.astype(narrow).reshape(dp_count, -1, query_wgrad.shape[1])
    query_wgrad = scatter_dp(query_wgrad, first_order)
    kv_up_grad = kv_up_grad.astype(narrow).reshape(dp_count, -1, kv_up_grad.shape[1])
    kv_up_grad = scatter_dp(kv_up_grad, second_order)
    tall = scatter_dp(tall, second_order).astype(narrow)
    tall = exchange(tall.reshape(tensor_count, -1, tall.shape[1]), TENSOR)
    tall = jnp.sum(tall.astype(wide), axis=0)
    kv_down_grad = tall[:, : LATENT + ROPE]
    router_grad = tall[:, LATENT + ROPE :]
    residual_all = all_in.astype(wide)
    gain_one_grad = jnp.sum(
        hidden_one_share * (residual_all * rms_scale(residual_all)), axis=0
    )
    devices = dp_count * tensor_count
    gain_grads = jnp.concatenate(
        [
            gain_one_grad.reshape(devices, -1),
            gain_two_grad.reshape(devices, -1),
            gain_lat_grad.reshape(devices, -1),
        ],
        axis=1,
    )
    gain_grads = jnp.sum(exchange(gain_grads, both), axis=0)
    return (
        block_out,
        input_grad,
        gain_grads[:split_one],
        query_wgrad,
        kv_down_grad,
        gain_grads[2 * split_one :],
        kv_up_grad,
        output_grad,
        gain_grads[split_one : 2 * split_one],
        router_grad,
        shared_grads[0],
        shared_grads[1],
        shared_grads[2],
        expert_gate_grad,
        expert_up_wgrad,
        expert_down_grad,
    )


def solution(mesh):
    in_specs = (
        P((DP, TENSOR), None),
        P((DP, TENSOR)),
        P(DP, TENSOR),
        P((DP, TENSOR), None),
        P((DP, TENSOR)),
        P(DP, TENSOR),
        P(TENSOR, DP),
        P((DP, TENSOR)),
        P((DP, TENSOR), None),
        P(DP, None),
        P(DP, TENSOR),
        P(DP, TENSOR),
        P(TENSOR, DP),
        P(None, DP, TENSOR),
        P(None, DP, TENSOR),
        P(None, TENSOR, DP),
        P((DP, TENSOR), None),
    )
    out_specs = (
        P((DP, TENSOR), None),
        P((DP, TENSOR), None),
        P((DP, TENSOR)),
        P(DP, TENSOR),
        P((DP, TENSOR), None),
        P((DP, TENSOR)),
        P(DP, TENSOR),
        P(TENSOR, DP),
        P((DP, TENSOR)),
        P((DP, TENSOR), None),
        P(DP, TENSOR),
        P(DP, TENSOR),
        P(TENSOR, DP),
        P(None, DP, TENSOR),
        P(None, DP, TENSOR),
        P(None, TENSOR, DP),
    )
    return jax.shard_map(block, mesh=mesh, in_specs=in_specs, out_specs=out_specs, check_vma=False)
```
